32 devices in a mesh: dp: 8 (over z, y), tensor: 4 (over x, core).
Axes of the slice: x: 2, y: 2, z: 4, core: 2. Of those that a mesh axis runs over, the one named last changes fastest.
Arguments:
- tokens: bfloat16 [8, 512, 768], P('dp'), may hold values from -6 to 6
- cotangent: bfloat16 [8, 512, 768], P('dp'), may hold values from -6 to 6
- norm_gain: float32 [768], replicated, may hold values from 0.1 to 1.9
- w_z: bfloat16 [768, 1536], P(None, 'tensor'), may hold values from -0.21875 to 0.21875
- w_x: bfloat16 [768, 1536], P(None, 'tensor'), may hold values from -0.21875 to 0.21875
- w_bc: bfloat16 [768, 256], replicated, may hold values from -0.21875 to 0.21875
- w_dt: bfloat16 [768, 24], P(None, 'tensor'), may hold values from -0.21875 to 0.21875
- conv_x: float32 [4, 1536], P(None, 'tensor'), may hold values from -3 to 3
- conv_x_bias: float32 [1536], P('tensor'), may hold values from -3 to 3
- conv_bc: float32 [4, 256], replicated, may hold values from -3 to 3
- conv_bc_bias: float32 [256], replicated, may hold values from -3 to 3
- dt_bias: float32 [24], P('tensor'), may hold values from -5 to -1
- a_log: float32 [24], P('tensor'), may hold values from -4 to 2
- d_skip: float32 [24], P('tensor'), may hold values from 0.5 to 2
- gate_gain: float32 [1536], P('tensor'), may hold values from 0.1 to 1.9
- w_out: bfloat16 [1536, 768], P('tensor'), may hold values from -0.15625 to 0.15625
Outputs:
- result: bfloat16 [8, 512, 768], P('dp')
- grad_x: bfloat16 [8, 512, 768], P('dp')
- grad_norm_gain: float32 [768], replicated
- grad_w_z: float32 [768, 1536], P(None, 'tensor')
- grad_w_x: float32 [768, 1536], P(None, 'tensor')
- grad_w_bc: float32 [768, 256], replicated
- grad_w_dt: float32 [768, 24], P(None, 'tensor')
- grad_conv_x: float32 [4, 1536], P(None, 'tensor')
- grad_conv_x_bias: float32 [1536], P('tensor')
- grad_conv_bc: float32 [4, 256], replicated
- grad_conv_bc_bias: float32 [256], replicated
- grad_dt_bias: float32 [24], P('tensor')
- grad_a_log: float32 [24], P('tensor')
- grad_d_skip: float32 [24], P('tensor')
- grad_gate_gain: float32 [1536], P('tensor')
- grad_w_out: float32 [1536, 768], P('tensor')
The draws below stay inside these ranges and needn't reach their ends.
All inputs are finite; a program needn't handle non-finite values.
Results may differ from the reference program's by a relative error of at most 0.013.
Values may be sent and summed in bfloat16 or wider, within the bound.
A program may use at most 128 MiB of HBM per device.

```python
import jax
import jax.numpy as jnp
from jax import lax

D = 768
H = 24
N = 128
K = 4
Q = 256
L = 512
DI = 1536
SEQS = 8


def shard_levels(stream_key, dims, cuts, least, high):
    def one(dim, blocks):
        steps = jax.random.uniform(jax.random.fold_in(jax.random.fold_in(stream_key, 6), dim), (blocks,), jnp.float32, least / len(cuts), high / len(cuts))
        return jnp.repeat(jnp.exp(steps), dims[dim] // blocks).reshape((-1,) + (1,) * (len(dims) - dim - 1))

    level = one(*cuts[0])
    for cut in cuts[1:]:
        level = level * one(*cut)
    return level


def centred(stream_key, dims, width, reach, split=(), held_as=jnp.bfloat16):
    level = shard_levels(stream_key, dims, split, -0.22, 0.18) if split else 1.0
    values = jax.random.normal(stream_key, dims, jnp.float32) * width * level
    return jnp.minimum(jnp.maximum(values, -reach), reach).astype(held_as)


def setup_inputs(seed: int = 0) -> dict:
    key_list = jax.random.split(jax.random.key(seed), 17)
    tokens = centred(key_list[0], (SEQS, L, D), 1.0, 6.0, ((0, 8),))
    cotangent = centred(key_list[1], (SEQS, L, D), 1.0, 6.0, ((0, 8),))
    norm_gain = jnp.clip(1.0 + 0.18 * jax.random.normal(key_list[2], (D,), jnp.float32), 0.1, 1.9)
    w_z = centred(key_list[3], (D, DI), D ** -0.5, 0.21875, ((1, 4),))
    w_x = centred(key_list[4], (D, DI), D ** -0.5, 0.21875, ((1, 4),))
    w_bc = centred(key_list[5], (D, 2 * N), D ** -0.5, 0.21875)
    w_dt = centred(key_list[6], (D, H), D ** -0.5, 0.21875, ((1, 4),))
    conv_x = centred(key_list[7], (K, DI), K ** -0.5, 3.0, ((1, 4),), jnp.float32)
    conv_x_bias = centred(key_list[8], (DI,), 0.5, 3.0, ((0, 4),), jnp.float32)
    conv_bc = centred(key_list[9], (K, 2 * N), K ** -0.5, 3.0, (), jnp.float32)
    conv_bc_bias = centred(key_list[10], (2 * N,), 0.5, 3.0, (), jnp.float32)
    dt_bias = jnp.clip(-5.0 + 4.0 * jax.random.uniform(key_list[11], (H,), jnp.float32) ** shard_levels(key_list[11], (H,), ((0, 4),), -0.2, 0.2), -5.0, -1.0)
    a_log = jnp.clip(-4.0 + 6.0 * jax.random.uniform(key_list[12], (H,), jnp.float32) ** shard_levels(key_list[12], (H,), ((0, 4),), -0.2, 0.2), -4.0, 2.0)
    d_skip = jnp.clip(0.5 + 1.5 * jax.random.uniform(key_list[13], (H,), jnp.float32) ** shard_levels(key_list[13], (H,), ((0, 4),), -0.2, 0.2), 0.5, 2.0)
    gate_gain = jnp.clip(1.0 + 0.18 * jax.random.normal(key_list[14], (DI,), jnp.float32), 0.1, 1.9)
    w_out = centred(key_list[15], (DI, D), DI ** -0.5, 0.15625, ((0, 4),))
    return {"tokens": tokens, "cotangent": cotangent, "norm_gain": norm_gain, "w_z": w_z, "w_x": w_x, "w_bc": w_bc, "w_dt": w_dt, "conv_x": conv_x, "conv_x_bias": conv_x_bias, "conv_bc": conv_bc, "conv_bc_bias": conv_bc_bias, "dt_bias": dt_bias, "a_log": a_log, "d_skip": d_skip, "gate_gain": gate_gain, "w_out": w_out}


epsilon = 1e-05
highest = lax.Precision.HIGHEST

def input_norm(values, norm_gain):
    return values * lax.rsqrt(lax.optimization_barrier(jnp.mean(values * values, axis=-1, keepdims=True)) + epsilon) * norm_gain[None, :]

def causal_conv(values, kernel, shift_bias):
    length = values.shape[0]
    kernel_taps = kernel.shape[0]
    padded = jnp.pad(values, ((kernel_taps - 1, 0), (0, 0)))
    summed = jnp.zeros_like(values) + shift_bias[None, :]
    for offset in range(kernel_taps):
        summed = summed + kernel[offset][None, :] * padded[offset:offset + length]
    return summed

def state_scan(xheads, b_rows, c_rows, step_size, log_decay):
    length, head_count, head_dim = xheads.shape
    blocks = length // Q
    states = b_rows.shape[1]
    causal_mask = jnp.arange(Q)[:, None] >= jnp.arange(Q)[None, :]

    def advance(carried_state, pieces):
        x_blk, b_blk, c_blk, dt_blk, a_blk = pieces
        cumulative = jnp.cumsum(a_blk, axis=0)
        spread = jnp.where(causal_mask[:, :, None], cumulative[:, None, :] - cumulative[None, :, :], -jnp.inf)
        scores = jnp.dot(c_blk, b_blk.T, precision=highest)
        mixing = scores[:, :, None] * jnp.exp(spread) * dt_blk[None, :, :]
        inside = jnp.einsum('tsh,shp->thp', mixing, x_blk, precision=highest)
        carried = jnp.einsum('tn,hpn->thp', c_blk, carried_state, precision=highest) * jnp.exp(cumulative)[:, :, None]
        weight_tail = jnp.exp(cumulative[-1][None, :] - cumulative) * dt_blk
        update = jnp.einsum('shp,sn->hpn', x_blk * weight_tail[:, :, None], b_blk, precision=highest)
        carried_state = carried_state * jnp.exp(cumulative[-1])[:, None, None] + update
        return (carried_state, inside + carried)
    initial = jnp.zeros((head_count, head_dim, states), jnp.float32)
    pieces = (xheads.reshape(blocks, Q, head_count, head_dim), b_rows.reshape(blocks, Q, states), c_rows.reshape(blocks, Q, states), step_size.reshape(blocks, Q, head_count), log_decay.reshape(blocks, Q, head_count))
    _, outputs = lax.scan(advance, initial, pieces)
    return outputs.reshape(length, head_count, head_dim)

def mixer(x_pre, bc_pre, dt_pre, conv_x, conv_x_bias, conv_bc, conv_bc_bias, dt_bias, a_log, d_skip):
    length, head_count = dt_pre.shape
    xconv = jax.nn.silu(causal_conv(x_pre, conv_x, conv_x_bias))
    bcconv = jax.nn.silu(causal_conv(bc_pre, conv_bc, conv_bc_bias))
    states = bc_pre.shape[1] // 2
    step_size = jax.nn.softplus(dt_pre + dt_bias[None, :])
    log_decay = -step_size * jnp.exp(a_log)[None, :]
    xheads = xconv.reshape(length, head_count, -1)
    mixed = state_scan(xheads, bcconv[:, :states], bcconv[:, states:], step_size, log_decay)
    mixed = mixed + d_skip[None, :, None] * xheads
    return mixed.reshape(length, -1)

def silu_slope(values):
    sigmoid = jax.nn.sigmoid(values)
    return sigmoid * (1.0 + values * (1.0 - sigmoid))

def contract_rows(left, right):
    return lax.dot_general(left, right, (((0,), (0,)), ((), ())), preferred_element_type=jnp.float32)

def contract_cols(left, right):
    return lax.dot_general(left, right, (((1,), (1,)), ((), ())), preferred_element_type=jnp.float32)

def sequence_pass(sequence, cotan, norm_gain, w_z, w_x, w_bc, w_dt, conv_x, conv_x_bias, conv_bc, conv_bc_bias, dt_bias, a_log, d_skip, gate_gain, w_out):
    widef = sequence.astype(jnp.float32)
    normed_f, norm_back = jax.vjp(input_norm, widef, norm_gain)
    normed = normed_f.astype(jnp.bfloat16)
    gate_pre = jnp.dot(normed, w_z, preferred_element_type=jnp.float32)
    x_pre = jnp.dot(normed, w_x, preferred_element_type=jnp.float32)
    bc_pre = jnp.dot(normed, w_bc, preferred_element_type=jnp.float32)
    dt_pre = jnp.dot(normed, w_dt, preferred_element_type=jnp.float32)
    mixed, mixer_back = jax.vjp(mixer, x_pre, bc_pre, dt_pre, conv_x, conv_x_bias, conv_bc, conv_bc_bias, dt_bias, a_log, d_skip)
    gate_act = jax.nn.silu(gate_pre)
    gated = mixed * gate_act
    inverse = lax.rsqrt(lax.optimization_barrier(jnp.mean(gated * gated, axis=-1, keepdims=True)) + epsilon)
    gated_n = (gated * inverse * gate_gain[None, :]).astype(jnp.bfloat16)
    result = (widef + jnp.dot(gated_n, w_out, preferred_element_type=jnp.float32)).astype(jnp.bfloat16)
    grad_w_out = contract_rows(gated_n, cotan)
    d_gated_n = contract_cols(cotan, w_out)
    grad_gate_gain = lax.optimization_barrier(jnp.sum(d_gated_n * gated * inverse, axis=0))
    scaled = gate_gain[None, :] * d_gated_n
    d_gated = inverse * scaled - gated * inverse ** 3 * lax.optimization_barrier(jnp.mean(scaled * gated, axis=-1, keepdims=True))
    d_mixed = d_gated * gate_act
    d_gate_pre = d_gated * mixed * silu_slope(gate_pre)
    back = mixer_back(d_mixed)
    d_gate_b = d_gate_pre.astype(jnp.bfloat16)
    d_x_b = back[0].astype(jnp.bfloat16)
    d_bc_b = back[1].astype(jnp.bfloat16)
    d_dt_b = back[2].astype(jnp.bfloat16)
    grad_w_z = contract_rows(normed, d_gate_b)
    grad_w_x = contract_rows(normed, d_x_b)
    grad_w_bc = contract_rows(normed, d_bc_b)
    grad_w_dt = contract_rows(normed, d_dt_b)
    d_normed = contract_cols(d_gate_b, w_z) + contract_cols(d_x_b, w_x) + contract_cols(d_bc_b, w_bc) + contract_cols(d_dt_b, w_dt)
    d_tokens, grad_norm_gain = norm_back(d_normed)
    grad_x = (cotan.astype(jnp.float32) + d_tokens).astype(jnp.bfloat16)
    grads = (grad_norm_gain, grad_w_z, grad_w_x, grad_w_bc, grad_w_dt, back[3], back[4], back[5], back[6], back[7], back[8], back[9], grad_gate_gain, grad_w_out)
    return (result, grad_x, grads)

def reference(tokens, cotangent, norm_gain, w_z, w_x, w_bc, w_dt, conv_x, conv_x_bias, conv_bc, conv_bc_bias, dt_bias, a_log, d_skip, gate_gain, w_out):
    params = (norm_gain, w_z, w_x, w_bc, w_dt, conv_x, conv_x_bias, conv_bc, conv_bc_bias, dt_bias, a_log, d_skip, gate_gain, w_out)
    zero_grads = (jnp.zeros(norm_gain.shape, jnp.float32), jnp.zeros(w_z.shape, jnp.float32), jnp.zeros(w_x.shape, jnp.float32), jnp.zeros(w_bc.shape, jnp.float32), jnp.zeros(w_dt.shape, jnp.float32), jnp.zeros(conv_x.shape, jnp.float32), jnp.zeros(conv_x_bias.shape, jnp.float32), jnp.zeros(conv_bc.shape, jnp.float32), jnp.zeros(conv_bc_bias.shape, jnp.float32), jnp.zeros(dt_bias.shape, jnp.float32), jnp.zeros(a_log.shape, jnp.float32), jnp.zeros(d_skip.shape, jnp.float32), jnp.zeros(gate_gain.shape, jnp.float32), jnp.zeros(w_out.shape, jnp.float32))

    def visit(totals, pair):
        result, grad_x, grads = sequence_pass(pair[0], pair[1], *params)
        totals = tuple((left + right for left, right in zip(totals, grads)))
        return (totals, (result, grad_x))
    totals, (results, grads_x) = lax.scan(visit, zero_grads, (tokens, cotangent))
    return (results, grads_x) + totals
```

```python
import functools

import jax
import jax.numpy as jnp
from jax import lax
from jax.experimental import pallas as pl
from jax.experimental.pallas import tpu as pltpu
from jax.sharding import PartitionSpec as P

Q = 256
LANES = 128
HEAD = 8
epsilon = 1e-05
highest = lax.Precision.HIGHEST
f32 = jnp.float32
bf16 = jnp.bfloat16
NN = ((1,), (0,))
NT = ((1,), (1,))
TN = ((0,), (0,))


def mm(a, b, dims=NN):
    return lax.dot_general(
        a.astype(bf16), b.astype(bf16), (dims, ((), ())), preferred_element_type=f32
    )


def exact(a, b, dims=NN):
    return lax.dot_general(a, b, (dims, ((), ())), precision=highest, preferred_element_type=f32)


def iota(shape, dim):
    return lax.broadcasted_iota(jnp.int32, shape, dim)


def spread_matrix(width, head_dim):
    return (iota((LANES, width), 1) // head_dim == iota((LANES, width), 0)).astype(f32)


def spread_rows(width, head_dim):
    return (iota((width, LANES), 0) // head_dim == iota((width, LANES), 1)).astype(f32)


def shifted(pad_ref, start, kernel_ref, bias_ref):
    taps = kernel_ref.shape[0]
    total = bias_ref + jnp.zeros((Q, pad_ref.shape[1]), f32)
    for j in range(taps):
        total = total + kernel_ref[j : j + 1, :] * pad_ref[pl.ds(HEAD + start - taps + 1 + j, Q), :]
    return total


def softplus(v):
    return jnp.maximum(v, 0.0) + jnp.log1p(jnp.exp(-jnp.abs(v)))


def decays(dt_rows, hp_ref):
    pre = dt_rows + hp_ref[0:1, :]
    step = softplus(pre)
    rate = jnp.exp(hp_ref[1:2, :])
    log_decay = -step * rate
    lower = (iota((Q, Q), 0) >= iota((Q, Q), 1)).astype(f32)
    return pre, step, rate, log_decay, exact(lower, log_decay)


def hp_skip_col(hp):
    wide = jnp.where(iota((LANES, LANES), 0) == iota((LANES, LANES), 1), hp[2:3, :], 0.0)
    return jnp.sum(wide, axis=1, keepdims=True)


def put_rows(ref, start, value):
    count = value.shape[1] // LANES
    for r in range(value.shape[0]):
        for k in range(count):
            at = start + r * count + k
            ref[at : at + 1, :] = value[r : r + 1, k * LANES : (k + 1) * LANES]
    return start + value.shape[0] * count


def get_row(ref, at, width):
    count = width // LANES
    return jnp.concatenate([ref[at + k : at + k + 1, :] for k in range(count)], axis=1)


class Scratch:
    def __init__(self):
        self.names, self.shapes = [], []

    def add(self, name, shape):
        self.names.append(name)
        self.shapes.append(shape)

    def vmem(self, name, shape, dtype=f32):
        self.add(name, pltpu.VMEM(shape, dtype))

    def dma(self, name, count):
        self.add(name, pltpu.SemaphoreType.DMA((count,)))

    def bind(self, refs):
        return dict(zip(self.names, refs))


def remote(src, dst, send, recv, k, peer):
    return pltpu.make_async_remote_copy(
        src_ref=src,
        dst_ref=dst,
        send_sem=send.at[k],
        recv_sem=recv.at[k],
        device_id=peer,
        device_id_type=pl.DeviceIdType.MESH,
    )


def rows_of(ref, start, rows, unit):
    if not isinstance(start, int):
        start = pl.multiple_of(start, unit)
    return ref.at[pl.ds(start, rows), :]


def add_to(target, a, b):
    target[...] = (a[...].astype(f32) + b[...].astype(f32)).astype(target.dtype)


class Place:
    def __init__(self):
        n = lax.axis_size("dp") // 2
        me = lax.axis_index("dp")
        self.n = n
        self.side = lax.rem(me, 2)
        pos = me // 2
        self.pair = {"dp": me + 1 - 2 * self.side}
        self.high = (pos >= n // 2).astype(jnp.int32)
        step = 2 * (1 - 2 * self.high)
        self.inner = {"dp": me + step}
        self.outer = {"dp": me - step}
        self.end = (pos == 0) | (pos == n - 1)
        self.mid = (pos == n // 2 - 1) | (pos == n // 2)
        self.has_outer = jnp.logical_not(self.end)
        self.below = jnp.logical_not(self.mid)


class PairFirst:
    copies = 5

    def __init__(self, sc, name, rows, lanes, dtype):
        self.name, self.rows = name, rows
        half = rows // 2
        self.unit = 32 // jnp.dtype(dtype).itemsize
        assert half % self.unit == 0
        for k in ("y", "acc", "in", "mid"):
            sc.vmem(name + k, (half, lanes), dtype)
        sc.dma(name + "s", self.copies)
        sc.dma(name + "r", self.copies)

    def run(self, s, at, src, out):
        half = self.rows // 2
        y, acc, slot, mid = (s[self.name + k] for k in ("y", "acc", "in", "mid"))
        send, recv = s[self.name + "s"], s[self.name + "r"]
        keep, give = at.side * half, (1 - at.side) * half
        mine = rows_of(src, keep, half, self.unit)
        done = rows_of(out, keep, half, self.unit)
        c_y = remote(rows_of(src, give, half, self.unit), y, send, recv, 0, at.pair)
        c_in = remote(acc, slot, send, recv, 1, at.inner)
        c_mid = remote(acc, mid, send, recv, 2, at.inner)
        c_out = remote(done, done, send, recv, 3, at.outer)
        c_back = remote(done, done, send, recv, 4, at.pair)
        c_y.start()
        yield
        c_y.wait()
        add_to(acc, mine, y)

        @pl.when(at.end & at.below)
        def _():
            c_in.start()

        yield

        @pl.when(at.has_outer)
        def _():
            c_in.wait_recv()
            add_to(acc, acc, slot)

        if at.n > 4:

            @pl.when(at.has_outer & at.below)
            def _():
                c_in.start()

        @pl.when(at.mid)
        def _():
            c_mid.start()

        yield

        @pl.when(at.mid)
        def _():
            c_mid.wait()
            add_to(done, acc, mid)
            c_back.start()

        @pl.when(at.mid & at.has_outer)
        def _():
            c_out.start()

        yield

        @pl.when(at.below)
        def _():
            c_in.wait_send()
            c_out.wait_recv()
            c_back.start()

        if at.n > 4:

            @pl.when(at.below & at.has_outer)
            def _():
                c_out.start()

        yield
        c_back.wait()

        @pl.when(at.has_outer)
        def _():
            c_out.wait_send()


class LineFirst:
    copies = 6

    def __init__(self, sc, name, rows, lanes, dtype):
        self.name, self.rows = name, rows
        half = rows // 2
        self.unit = 32 // jnp.dtype(dtype).itemsize
        assert half % self.unit == 0
        for k in ("acc", "in"):
            sc.vmem(name + k, (rows, lanes), dtype)
        for k in ("mid", "y"):
            sc.vmem(name + k, (half, lanes), dtype)
        sc.dma(name + "s", self.copies)
        sc.dma(name + "r", self.copies)

    def run(self, s, at, src, out):
        half = self.rows // 2
        acc, slot, mid, y = (s[self.name + k] for k in ("acc", "in", "mid", "y"))
        send, recv = s[self.name + "s"], s[self.name + "r"]
        own, other = at.high * half, (1 - at.high) * half
        acc_own = rows_of(acc, own, half, self.unit)
        acc_other = rows_of(acc, other, half, self.unit)
        out_own = rows_of(out, own, half, self.unit)
        out_other = rows_of(out, other, half, self.unit)
        c_end = remote(src, slot, send, recv, 0, at.inner)
        c_in = remote(acc, slot, send, recv, 0, at.inner)
        c_mid = remote(acc_other, mid, send, recv, 1, at.inner)
        c_y = remote(acc_own, y, send, recv, 2, at.pair)
        c_out = remote(out_own, out_own, send, recv, 3, at.outer)
        c_back = remote(out_own, out_own, send, recv, 4, at.inner)
        c_out2 = remote(out_other, out_other, send, recv, 5, at.outer)
        if at.n == 2:
            acc[...] = src[...]
        else:

            @pl.when(at.end)
            def _():
                c_end.start()

        yield

        @pl.when(at.has_outer)
        def _():
            c_in.wait_recv()
            add_to(acc, src, slot)

        if at.n > 4:

            @pl.when(at.has_outer & at.below)
            def _():
                c_in.start()

        @pl.when(at.mid)
        def _():
            c_mid.start()

        yield

        @pl.when(at.mid)
        def _():
            c_mid.wait()
            add_to(acc_own, acc_own, mid)
            c_y.start()

        yield

        @pl.when(at.mid)
        def _():
            c_y.wait()
            add_to(out_own, acc_own, y)
            c_back.start()

        @pl.when(at.mid & at.has_outer)
        def _():
            c_out.start()

        yield

        @pl.when(at.mid)
        def _():
            c_back.wait_recv()

        @pl.when(at.mid & at.has_outer)
        def _():
            c_out2.start()

        yield

        @pl.when(at.below)
        def _():
            c_in.wait_send()
            c_out.wait_recv()

        if at.n > 4:

            @pl.when(at.below & at.has_outer)
            def _():
                c_out.start()

        @pl.when(at.below)
        def _():
            c_out2.wait_recv()

        if at.n > 4:

            @pl.when(at.below & at.has_outer)
            def _():
                c_out2.start()

        @pl.when(at.mid)
        def _():
            c_back.wait_send()

        @pl.when(at.has_outer)
        def _():
            c_out.wait_send()
            c_out2.wait_send()


def flip(axis, bit):
    me = lax.axis_index(axis)
    side = lax.rem(me // bit, 2)
    return side, {axis: me + bit - 2 * bit * side}


class Halves:
    def __init__(self, sc, name, rows, lanes, dtype, bits):
        self.name, self.rows, self.bits = name, rows, bits
        half = rows // 2
        self.unit = 32 // jnp.dtype(dtype).itemsize
        assert half % self.unit == 0
        for k in range(len(bits)):
            sc.vmem(f"{name}slot{k}", (half, lanes), dtype)
        for k in range(len(bits) - 1):
            sc.vmem(f"{name}acc{k}", (half, lanes), dtype)
        sc.dma(name + "s", len(bits) + 1)
        sc.dma(name + "r", len(bits) + 1)

    def run(self, s, at, src, out):
        half, last = self.rows // 2, len(self.bits) - 1
        send, recv = s[self.name + "s"], s[self.name + "r"]
        side, peer = flip(*self.bits[0])
        keep, give = side * half, (1 - side) * half
        done = rows_of(out, keep, half, self.unit)
        mine = rows_of(src, keep, half, self.unit)
        copy = remote(
            rows_of(src, give, half, self.unit), s[f"{self.name}slot0"], send, recv, 0, peer
        )
        copy.start()
        for k in range(last + 1):
            yield
            copy.wait()
            target = done if k == last else s[f"{self.name}acc{k}"]
            add_to(target, mine, s[f"{self.name}slot{k}"])
            if k < last:
                mine = target
                copy = remote(
                    mine, s[f"{self.name}slot{k + 1}"], send, recv, k + 1, flip(*self.bits[k + 1])[1]
                )
            else:
                copy = remote(done, done, send, recv, last + 1, peer)
            copy.start()
        yield
        copy.wait()


class Nested:
    def __init__(self, sc, name, rows, lanes, dtype, bits, inner):
        self.name, self.bits = name, bits
        self.unit = 32 // jnp.dtype(dtype).itemsize
        self.sizes = [rows >> k for k in range(len(bits) + 1)]
        for k in range(len(bits)):
            sc.vmem(f"{name}slot{k}", (self.sizes[k + 1], lanes), dtype)
            sc.vmem(f"{name}acc{k}", (self.sizes[k + 1], lanes), dtype)
        sc.dma(name + "s", 2 * len(bits))
        sc.dma(name + "r", 2 * len(bits))
        self.inner = inner(sc, name + "i", self.sizes[-1], lanes, dtype)

    def run(self, s, at, src, out):
        send, recv = s[self.name + "s"], s[self.name + "r"]
        off, trail, ref = 0, [], src
        for k, bit in enumerate(self.bits):
            half = self.sizes[k + 1]
            side, peer = flip(*bit)
            keep, give = side * half, (1 - side) * half
            slot, acc = s[f"{self.name}slot{k}"], s[f"{self.name}acc{k}"]
            copy = remote(rows_of(ref, give, half, self.unit), slot, send, recv, k, peer)
            copy.start()
            yield
            copy.wait()
            add_to(acc, rows_of(ref, keep, half, self.unit), slot)
            trail.append((off, peer))
            off, ref = off + keep, acc
        yield from self.inner.run(s, at, ref, rows_of(out, off, self.sizes[-1], self.unit))
        count = len(self.bits)
        for k in reversed(range(count)):
            parent, peer = trail[k]
            part = rows_of(out, off, self.sizes[k + 1], self.unit)
            copy = remote(part, part, send, recv, count + k, peer)
            copy.start()
            yield
            copy.wait()
            off = parent


class Small:
    def __init__(self, sc, name, rows, lanes, extra, bits):
        self.name, self.rows, self.extra, self.bits = name, rows, extra, bits
        for k in range(len(bits)):
            sc.vmem(f"{name}slot{k}", (extra, lanes), f32)
            sc.vmem(f"{name}acc{k}", (extra, lanes), f32)
        sc.dma(name + "s", len(bits))
        sc.dma(name + "r", len(bits))
        self.inner = PairFirst(sc, name + "i", rows + extra, lanes, f32)

    def run(self, s, at, src, out):
        send, recv = s[self.name + "s"], s[self.name + "r"]
        tail = src.at[pl.ds(self.rows, self.extra), :]
        ref = tail
        for k, bit in enumerate(self.bits):
            slot, acc = s[f"{self.name}slot{k}"], s[f"{self.name}acc{k}"]
            copy = remote(ref, slot, send, recv, k, flip(*bit)[1])
            copy.start()
            yield
            copy.wait()
            add_to(acc, ref, slot)
            ref = acc
        tail[...] = ref[...]
        yield from self.inner.run(s, at, src, out)


def greet(at, bits):
    barrier = pltpu.get_barrier_semaphore()

    def hello(peer):
        pl.semaphore_signal(
            barrier, inc=1, device_id=peer, device_id_type=pl.DeviceIdType.MESH
        )

    size = lax.axis_size("tensor")
    me = lax.axis_index("tensor")
    for d in range(1, size):
        hello({"tensor": lax.rem(me + d, size)})
    hello(at.pair)
    hello(at.inner)

    @pl.when(at.has_outer)
    def _():
        hello(at.outer)

    def meet():
        pl.semaphore_wait(barrier, size + 1 + at.has_outer.astype(jnp.int32))

    return meet


def exchange(s, c, stats):
    size = lax.axis_size("tensor")
    me = lax.axis_index("tensor")
    copies = []
    for d in range(1, size):
        k = c * (size - 1) + d - 1
        copy = remote(
            stats.at[c], s["st_slot"].at[k], s["st_s"], s["st_r"], k, {"tensor": lax.rem(me + d, size)}
        )
        copy.start()
        copies.append((copy, k))
    return copies


def front(heads, a, s, ready, meet):
    length, inner = s["mixed"].shape
    states = a["cbc"].shape[1] // 2
    head_dim = inner // heads
    per = LANES // head_dim
    chunks = length // Q
    hp, x_o, bc_o, state_o = s["hp"], s["x"], s["bc"], s["state"]
    wdt_s = s["wdt"]
    spread = spread_matrix(inner, head_dim)
    x_o[0:HEAD, :] = jnp.zeros((HEAD, inner), f32)
    bc_o[0:HEAD, :] = jnp.zeros((HEAD, 2 * states), f32)
    hp[...] = jnp.zeros(hp.shape, f32)
    wdt_s[...] = jnp.zeros(wdt_s.shape, bf16)
    causal = iota((Q, Q), 0) >= iota((Q, Q), 1)
    lane = iota((Q, LANES), 1)
    ready("tok", "ng")
    for c in range(chunks):
        rows = pl.ds(c * Q, Q)
        t = a["tok"][rows, :].astype(f32)
        n = t * lax.rsqrt(jnp.mean(t * t, axis=-1, keepdims=True) + epsilon) * row(a["ng"])
        s["normed"][rows, :] = n.astype(bf16)
    ready("dtw", "dtb", "alog", "dskip", "wbc")
    wdt_s[0:heads, :] = a["dtw"][...]
    for k, name in enumerate(("dtb", "alog", "dskip")):
        hp[k : k + 1, 0:heads] = row(a[name])
    for c in range(chunks):
        rows = pl.ds(c * Q, Q)
        n = s["normed"][rows, :]
        bc_o[pl.ds(HEAD + c * Q, Q), :] = mm(n, a["wbc"][...])
        s["dt"][rows, :] = mm(n, wdt_s[...], NT)
    ready("wx")
    for c in range(chunks):
        x_o[pl.ds(HEAD + c * Q, Q), :] = mm(s["normed"][pl.ds(c * Q, Q), :], a["wx"][...])
    ready("wz", "wo", "cot")
    for c in range(chunks):
        rows = pl.ds(c * Q, Q)
        s["gate"][rows, :] = mm(s["normed"][rows, :], a["wz"][...])
        s["dgn"][rows, :] = mm(a["cot"][rows, :], a["wo"][...], NT)
    ready("cx", "cxb", "cbc", "cbcb", "gg")
    copies = []
    for c in range(chunks):
        rows = pl.ds(c * Q, Q)
        v = shifted(x_o, c * Q, a["cx"], row(a["cxb"]))
        xc = v * jax.nn.sigmoid(v)
        v = shifted(bc_o, c * Q, a["cbc"], row(a["cbcb"]))
        bcc = v * jax.nn.sigmoid(v)
        b = bcc[:, :states].astype(bf16)
        cc = bcc[:, states:].astype(bf16)
        _, step, _, _, cum = decays(s["dt"][rows, :], hp)
        s["cum"][rows, :] = cum
        cum_t = jnp.transpose(cum)
        u = xc * exact(step, spread)
        scores = mm(cc, b, NT)
        outs = []
        for g in range(inner // LANES):
            part = u[:, g * LANES : (g + 1) * LANES]
            acc = jnp.zeros((Q, LANES), f32)
            for k in range(per):
                h = g * per + k
                e = jnp.exp(jnp.where(causal, cum[:, h : h + 1] - cum_t[h : h + 1, :], -1e30))
                acc = acc + mm(scores * e, jnp.where(lane // head_dim == k, part, 0.0))
            outs.append(acc)
        mixed = jnp.concatenate(outs, axis=1)
        if c > 0:
            mixed = mixed + mm(cc, state_o[c], NT) * exact(jnp.exp(cum), spread)
        if c + 1 < chunks:
            last = cum[Q - 1 : Q, :]
            tail = u * exact(jnp.exp(last - cum), spread)
            update = mm(tail, b, TN)
            if c > 0:
                rowdec = jnp.sum(
                    spread_rows(inner, head_dim) * jnp.exp(last), axis=1, keepdims=True
                )
                update = update + state_o[c] * rowdec
            state_o[c + 1] = update
        skip = jnp.sum(spread * hp_skip_col(hp), axis=0, keepdims=True)
        mixed = mixed + skip * xc
        s["mixed"][rows, :] = mixed
        gate = s["gate"][rows, :]
        gated = mixed * (gate * jax.nn.sigmoid(gate))
        sq = jnp.sum(gated * gated, axis=1, keepdims=True)
        pr = jnp.sum(row(a["gg"]) * s["dgn"][rows, :] * gated, axis=1, keepdims=True)
        both = jnp.where(lane == 0, sq, jnp.where(lane == 1, pr, 0.0))
        s["stats"][c] = jnp.transpose(both)[0:8, :]
        if c == 0:
            meet()
        copies.append(exchange(s, c, s["stats"]))
    return copies


def row(ref):
    return ref[...][None, :]


def back(heads, inner_total, a, s, copies, launch, hook):
    length, inner = s["mixed"].shape
    states = a["cbc"].shape[1] // 2
    head_dim = inner // heads
    per = LANES // head_dim
    taps = a["cx"].shape[0]
    chunks = length // Q
    hp, wdt_s = s["hp"], s["wdt"]
    x_r, bc_r = s["x"], s["bc"]
    gn_s, dz_s, dx_s, dbc_s, ddt_s = s["gn"], s["dz"], s["dx"], s["dbc"], s["ddt"]
    dvx_s, dvbc_s = s["dvx"], s["dvbc"]
    cx, cbc = a["cx"], a["cbc"]
    gg = row(a["gg"])
    spread = spread_matrix(inner, head_dim)
    spread_r = spread_rows(inner, head_dim)
    causal = iota((Q, Q), 0) >= iota((Q, Q), 1)
    lower = causal.astype(f32)
    lane = iota((Q, LANES), 1)
    skip = jnp.sum(spread * hp_skip_col(hp), axis=0, keepdims=True)
    dvx_s[pl.ds(length, HEAD), :] = jnp.zeros((HEAD, inner), f32)
    dvbc_s[pl.ds(length, HEAD), :] = jnp.zeros((HEAD, 2 * states), f32)
    g_gain = jnp.zeros((1, inner), f32)
    for c in range(chunks):
        rows = pl.ds(c * Q, Q)
        total = s["stats"][c]
        for copy, k in copies[c]:
            copy.wait()
            total = total + s["st_slot"][k]
        block = jnp.concatenate([total, jnp.zeros((LANES - 8, Q), f32)], axis=0)
        turned = jnp.transpose(block)
        gate = s["gate"][rows, :]
        mixed = s["mixed"][rows, :]
        sg = jax.nn.sigmoid(gate)
        act = gate * sg
        gated = mixed * act
        inv = lax.rsqrt(turned[:, 0:1] / inner_total + epsilon)
        pm = turned[:, 1:2] / inner_total
        dgn = s["dgn"][rows, :]
        normal = gated * inv
        gn_s[rows, :] = (normal * gg).astype(bf16)
        g_gain = g_gain + jnp.sum(dgn * normal, axis=0, keepdims=True)
        dg = inv * (gg * dgn) - gated * (inv * inv * inv) * pm
        s["dy"][rows, :] = dg * act
        dz_s[rows, :] = (dg * mixed * (sg * (1.0 + gate * (1.0 - sg)))).astype(bf16)
    s["p_gwo"][...] = mm(gn_s[...], a["cot"][...], TN).astype(bf16)
    launch("gwo")
    s["p_gz"][...] = mm(s["normed"][...], dz_s[...], TN).astype(bf16)
    launch("gz")
    s["p_res"][...] = mm(gn_s[...], a["wo"][...]).astype(bf16)
    launch("res")

    g_skip = jnp.zeros((1, inner), f32)
    g_alog = jnp.zeros((1, LANES), f32)
    g_dtb = jnp.zeros((1, LANES), f32)
    g_cx = [jnp.zeros((1, inner), f32) for _ in range(taps)]
    g_cxb = jnp.zeros((1, inner), f32)
    g_cbc = [jnp.zeros((1, 2 * states), f32) for _ in range(taps)]
    g_cbcb = jnp.zeros((1, 2 * states), f32)
    d_state = None
    for c in reversed(range(chunks)):
        rows = pl.ds(c * Q, Q)
        dy = s["dy"][rows, :]
        vx = shifted(x_r, c * Q, cx, row(a["cxb"]))
        sx = jax.nn.sigmoid(vx)
        xc = vx * sx
        vb = shifted(bc_r, c * Q, cbc, row(a["cbcb"]))
        sb = jax.nn.sigmoid(vb)
        bcc = vb * sb
        b = bcc[:, :states].astype(bf16)
        cc = bcc[:, states:].astype(bf16)
        pre = s["dt"][rows, :] + hp[0:1, :]
        step = softplus(pre)
        rate = jnp.exp(hp[1:2, :])
        log_decay = -step * rate
        cum = s["cum"][rows, :]
        cum_t = jnp.transpose(cum)
        stepw = exact(step, spread)
        u = xc * stepw
        scores = mm(cc, b, NT)
        d_scores = jnp.zeros((Q, Q), f32)
        d_cum = jnp.zeros((Q, LANES), f32)
        cols = jnp.zeros((8, Q), f32)
        dus = []
        for g in range(inner // LANES):
            up = u[:, g * LANES : (g + 1) * LANES].astype(bf16)
            dyp = dy[:, g * LANES : (g + 1) * LANES]
            acc = jnp.zeros((Q, LANES), f32)
            for k in range(per):
                h = g * per + k
                e = jnp.exp(jnp.where(causal, cum[:, h : h + 1] - cum_t[h : h + 1, :], -1e30))
                p = scores * e
                dyh = jnp.where(lane // head_dim == k, dyp, 0.0).astype(bf16)
                dp = mm(dyh, up, NT)
                d_scores = d_scores + dp * e
                gp = dp * p
                d_cum = d_cum + jnp.where(lane == h, jnp.sum(gp, axis=1, keepdims=True), 0.0)
                cols = cols + jnp.where(
                    iota((8, Q), 0) == h, jnp.sum(gp, axis=0, keepdims=True), 0.0
                )
                acc = acc + mm(p, dyh, TN)
            dus.append(acc)
            hook()
        du = jnp.concatenate(dus, axis=1)
        d_cum = d_cum - jnp.transpose(
            jnp.concatenate([cols, jnp.zeros((LANES - 8, Q), f32)], axis=0)
        )
        d_c = mm(d_scores, b)
        d_b = mm(d_scores, cc, TN)
        d_prev = None
        if c > 0:
            state = s["state"][c]
            decayed = exact(jnp.exp(cum), spread)
            dz = dy * decayed
            carried = mm(cc, state, NT) * dz
            d_cum = d_cum + exact(carried, spread, NT)
            d_c = d_c + mm(dz, state)
            d_prev = mm(dz, cc, TN)
        if d_state is not None:
            last = cum[Q - 1 : Q, :]
            tailw = exact(jnp.exp(last - cum), spread)
            ut = u * tailw
            dut = mm(b, d_state, NT)
            d_b = d_b + mm(ut, d_state)
            du = du + dut * tailw
            q = exact(dut * ut, spread, NT)
            d_last = jnp.sum(q, axis=0, keepdims=True)
            if c > 0:
                rowdec = jnp.sum(spread_r * jnp.exp(last), axis=1, keepdims=True)
                r = jnp.sum(d_state * s["state"][c], axis=1, keepdims=True) * rowdec
                d_last = d_last + jnp.sum(spread_r * r, axis=0, keepdims=True)
                d_prev = d_prev + d_state * rowdec
            d_cum = d_cum - q + jnp.where(iota((Q, LANES), 0) == Q - 1, d_last, 0.0)
        d_state = d_prev
        d_log = exact(lower, d_cum, TN)
        g_alog = g_alog + jnp.sum(d_log * log_decay, axis=0, keepdims=True)
        d_step = exact(du * xc, spread, NT) - d_log * rate
        d_pre = d_step * jax.nn.sigmoid(pre)
        d_pre = jnp.where(lane < heads, d_pre, 0.0)
        g_dtb = g_dtb + jnp.sum(d_pre, axis=0, keepdims=True)
        g_skip = g_skip + jnp.sum(dy * xc, axis=0, keepdims=True)
        dxc = du * stepw + skip * dy
        dvx = dxc * (sx * (1.0 + vx * (1.0 - sx)))
        dvb = jnp.concatenate([d_b, d_c], axis=1) * (sb * (1.0 + vb * (1.0 - sb)))
        dvx_s[rows, :] = dvx
        dvbc_s[rows, :] = dvb
        g_cxb = g_cxb + jnp.sum(dvx, axis=0, keepdims=True)
        g_cbcb = g_cbcb + jnp.sum(dvb, axis=0, keepdims=True)
        dx = jnp.zeros((Q, inner), f32)
        dbc = jnp.zeros((Q, 2 * states), f32)
        for j in range(taps):
            behind = pl.ds(c * Q + taps - 1 - j, Q)
            ahead = pl.ds(HEAD + c * Q - taps + 1 + j, Q)
            dx = dx + cx[j : j + 1, :] * dvx_s[behind, :]
            dbc = dbc + cbc[j : j + 1, :] * dvbc_s[behind, :]
            g_cx[j] = g_cx[j] + jnp.sum(dvx * x_r[ahead, :], axis=0, keepdims=True)
            g_cbc[j] = g_cbc[j] + jnp.sum(dvb * bc_r[ahead, :], axis=0, keepdims=True)
        dx_s[rows, :] = dx.astype(bf16)
        dbc_s[rows, :] = dbc.astype(bf16)
        ddt_s[rows, :] = d_pre.astype(bf16)
        hook()

    normed = s["normed"]
    s["p_gbc"][...] = mm(normed[...], dbc_s[...], TN).astype(bf16)
    launch("gbc")
    s["p_gx"][...] = mm(normed[...], dx_s[...], TN).astype(bf16)
    launch("gx")
    g_ng = jnp.zeros((1, normed.shape[1]), f32)
    for c in range(chunks):
        rows = pl.ds(c * Q, Q)
        dn = mm(dz_s[rows, :], a["wz"][...], NT) + mm(dx_s[rows, :], a["wx"][...], NT)
        dn = dn + mm(dbc_s[rows, :], a["wbc"][...], NT) + mm(ddt_s[rows, :], wdt_s[...])
        s["p_dn"][rows, :] = dn.astype(bf16)
        t = a["tok"][rows, :].astype(f32)
        unit = t * lax.rsqrt(jnp.mean(t * t, axis=-1, keepdims=True) + epsilon)
        g_ng = g_ng + jnp.sum(dn * unit, axis=0, keepdims=True)
    launch("dn")
    gdt = mm(ddt_s[...], normed[...], TN)
    small = s["p_sm"]
    small[...] = jnp.zeros(small.shape, f32)
    at = put_rows(small, 0, gdt[0:heads, :])
    for value in (*g_cx, g_cxb, g_gain, g_dtb, g_alog, exact(g_skip, spread, NT)):
        at = put_rows(small, at, value)
    at = -(-at // 8) * 8
    for value in (*g_cbc, g_cbcb, g_ng):
        at = put_rows(small, at, value)
    launch("sm")


INPUTS = (
    "tok", "cot", "ng", "wz", "wx", "wbc", "dtw", "cx", "cxb", "cbc", "cbcb",
    "dtb", "alog", "dskip", "gg", "wo",
)
FETCH = (
    "tok", "ng", "dtw", "dtb", "alog", "dskip", "wbc", "wx", "wz", "wo", "cot",
    "cx", "cxb", "cbc", "cbcb", "gg",
)
RESULTS = ("res", "dn", "gz", "gx", "gwo", "gbc", "sm")


def kernel_main(heads, inner_total, sc, plan, hooks, bits, *refs):
    hbm = dict(zip(INPUTS, refs))
    outs = dict(zip(RESULTS, refs[len(INPUTS) :]))
    s = sc.bind(refs[len(INPUTS) + len(RESULTS) :])
    at = Place()
    a = {name: s["a_" + name] for name in INPUTS}
    loads = {}
    for k, name in enumerate(FETCH):
        loads[name] = pltpu.make_async_copy(hbm[name], a[name], s["loads"].at[k])
        loads[name].start()
    meet = greet(at, bits)

    def ready(*names):
        for name in names:
            loads[name].wait()

    running = []

    def launch(name):
        for stream, source, start, rows in plan:
            if source == name:
                run = stream.run(
                    s,
                    at,
                    s["p_" + name].at[pl.ds(start, rows), :],
                    outs[name].at[pl.ds(start, rows), :],
                )
                next(run)
                running.append([stream.name, run, True])

    def advance(name):
        for entry in running:
            if entry[2] and entry[0] == name:
                entry[2] = next(entry[1], 1) is None

    turn = iter(hooks)

    def hook():
        for name in next(turn, ()):
            advance(name)

    copies = front(heads, a, s, ready, meet)
    back(heads, inner_total, a, s, copies, launch, hook)
    for names in turn:
        for name in names:
            advance(name)
    while any(entry[2] for entry in running):
        for entry in running:
            if entry[2]:
                entry[2] = next(entry[1], 1) is None


def kernel_finish(
    heads, taps, tok, cot, ng, a_res, a_dn, a_gz, a_gx, a_gwo, a_gbc, a_sm,
    res_o, gt_o, ng_o, gz_o, gx_o, gbc_o, gdt_o, cx_o, cxb_o, cbc_o, cbcb_o,
    dtb_o, alog_o, skip_o, gain_o, gwo_o,
):
    for c in range(tok.shape[0] // Q):
        rows = pl.ds(c * Q, Q)
        t = tok[rows, :].astype(f32)
        res_o[rows, :] = (t + a_res[rows, :].astype(f32)).astype(bf16)
        r = lax.rsqrt(jnp.mean(t * t, axis=-1, keepdims=True) + epsilon)
        gd = a_dn[rows, :].astype(f32) * row(ng)
        mean = jnp.mean(t * gd, axis=-1, keepdims=True)
        d = r * gd - t * (r * r * r) * mean
        gt_o[rows, :] = (cot[rows, :].astype(f32) + d).astype(bf16)
    gz_o[...] = a_gz[...].astype(f32)
    gx_o[...] = a_gx[...].astype(f32)
    gwo_o[...] = a_gwo[...].astype(f32)
    gbc_o[...] = a_gbc[...].astype(f32)
    at = 0
    for out in (gdt_o, cx_o):
        for r in range(out.shape[0]):
            out[r : r + 1, :] = get_row(a_sm, at, out.shape[1])
            at += out.shape[1] // LANES
    for out in (cxb_o, gain_o):
        out[...] = get_row(a_sm, at, out.shape[0])[0]
        at += out.shape[0] // LANES
    for out in (dtb_o, alog_o, skip_o):
        out[...] = a_sm[at, 0 : out.shape[0]]
        at += 1
    at = -(-at // 8) * 8
    for r in range(cbc_o.shape[0]):
        cbc_o[r : r + 1, :] = get_row(a_sm, at, cbc_o.shape[1])
        at += cbc_o.shape[1] // LANES
    for out in (cbcb_o, ng_o):
        out[...] = get_row(a_sm, at, out.shape[0])[0]
        at += out.shape[0] // LANES


def call(body, args, outs, scratch=(), limit=40, space=pltpu.VMEM, **params):
    vmem = pl.BlockSpec(memory_space=pltpu.VMEM)
    return pl.pallas_call(
        body,
        out_shape=[jax.ShapeDtypeStruct(s, d) for s, d in outs],
        in_specs=[pl.BlockSpec(memory_space=space) for _ in args],
        out_specs=[vmem] * len(outs),
        scratch_shapes=list(scratch),
        compiler_params=pltpu.CompilerParams(vmem_limit_bytes=limit * 1024 * 1024, **params),
    )(*args)


def per_device(
    tokens, cotangent, norm_gain, w_z, w_x, w_bc, w_dt, conv_x, conv_x_bias, conv_bc,
    conv_bc_bias, dt_bias, a_log, d_skip, gate_gain, w_out,
):
    seqs, length, width = tokens.shape
    assert seqs == 1 and length % Q == 0
    heads = dt_bias.shape[0]
    inner = w_z.shape[1]
    wide = w_bc.shape[1]
    states = wide // 2
    taps = conv_x.shape[0]
    dp, tensor = lax.axis_size("dp"), lax.axis_size("tensor")
    assert dp % 4 == 0 and tensor & (tensor - 1) == 0
    inner_total = inner * tensor
    chunks = length // Q
    tok = tokens.reshape(length, width)
    cot = cotangent.reshape(length, width)
    args = (
        tok, cot, norm_gain, w_z, w_x, w_bc, w_dt.T, conv_x, conv_x_bias, conv_bc,
        conv_bc_bias, dt_bias, a_log, d_skip, gate_gain, w_out,
    )
    bits = [("tensor", 1 << k) for k in range(tensor.bit_length() - 1)]
    sc = Scratch()
    for name, value in zip(INPUTS, args):
        sc.vmem("a_" + name, value.shape, value.dtype)
    sc.dma("loads", len(INPUTS))
    sc.vmem("wdt", (LANES, width), bf16)
    sc.vmem("hp", (8, LANES))
    sc.vmem("normed", (length, width), bf16)
    for name in ("gate", "mixed", "dgn", "dy"):
        sc.vmem(name, (length, inner))
    for name in ("x", "dvx"):
        sc.vmem(name, (length + HEAD, inner))
    for name in ("bc", "dvbc"):
        sc.vmem(name, (length + HEAD, wide))
    for name in ("dt", "cum"):
        sc.vmem(name, (length, LANES))
    sc.vmem("state", (chunks, inner, states))
    sc.vmem("stats", (chunks, 8, Q))
    sc.vmem("st_slot", (chunks * (tensor - 1), 8, Q))
    sc.dma("st_s", chunks * (tensor - 1))
    sc.dma("st_r", chunks * (tensor - 1))
    for name in ("gn", "dz", "dx"):
        sc.vmem(name, (length, inner), bf16)
    sc.vmem("dbc", (length, wide), bf16)
    sc.vmem("ddt", (length, LANES), bf16)
    own_rows = heads * width // LANES + (taps + 2) * inner // LANES + 3
    own_rows = -(-own_rows // 8) * 8
    all_rows = (taps + 1) * wide // LANES + width // LANES
    all_rows = -(-(own_rows + all_rows) // 16) * 16 - own_rows
    results = [
        ((length, width), bf16),
        ((length, width), bf16),
        ((width, inner), bf16),
        ((width, inner), bf16),
        ((inner, width), bf16),
        ((width, wide), bf16),
        ((own_rows + all_rows, LANES), f32),
    ]
    for name, (shape, dtype) in zip(RESULTS, results):
        sc.vmem("p_" + name, shape, dtype)
    plan = []

    def split(name, kinds):
        shape, dtype = results[RESULTS.index(name)]
        rows = shape[0] // len(kinds)
        for k, kind in enumerate(kinds):
            plan.append((kind(sc, f"{name}{k}", rows, shape[1], dtype), name, k * rows, rows))

    split("gwo", (PairFirst, LineFirst))
    split("gz", (PairFirst, LineFirst))
    split("gx", (PairFirst, LineFirst, PairFirst, LineFirst))
    for name in ("res", "dn"):
        shape, dtype = results[RESULTS.index(name)]
        plan.append((Halves(sc, name, *shape, dtype, bits), name, 0, shape[0]))
    plan.append((Nested(sc, "gbc", width, wide, bf16, bits, PairFirst), "gbc", 0, width))
    plan.append((Small(sc, "sm", own_rows, LANES, all_rows, bits), "sm", 0, own_rows + all_rows))
    hooks = [
        (),
        ("res",),
        ("gwo0",),
        ("gwo1", "gz0"),
        ("gwo0",),
        ("gwo1",),
        ("gwo0", "gz0"),
        ("gz1",),
    ]
    sums = call(
        functools.partial(kernel_main, heads, inner_total, sc, plan, hooks, bits),
        args,
        results,
        sc.shapes,
        limit=52,
        space=pltpu.HBM,
        collective_id=0,
        has_side_effects=True,
    )
    outs = call(
        functools.partial(kernel_finish, heads, taps),
        (tok, cot, norm_gain, *sums),
        [
            ((length, width), bf16),
            ((length, width), bf16),
            ((width,), f32),
            ((width, inner), f32),
            ((width, inner), f32),
            ((width, wide), f32),
            ((heads, width), f32),
            ((taps, inner), f32),
            ((inner,), f32),
            ((taps, wide), f32),
            ((wide,), f32),
            ((heads,), f32),
            ((heads,), f32),
            ((heads,), f32),
            ((inner,), f32),
            ((inner, width), f32),
        ],
        limit=32,
    )
    outs = list(outs)
    for k in range(2):
        outs[k] = outs[k].reshape(seqs, length, width)
    outs[6] = outs[6].T
    return tuple(outs)


def solution(mesh):
    placed = (
        P("dp", None, None),
        P("dp", None, None),
        P(),
        P(None, "tensor"),
        P(None, "tensor"),
        P(),
        P(None, "tensor"),
        P(None, "tensor"),
        P("tensor"),
        P(),
        P(),
        P("tensor"),
        P("tensor"),
        P("tensor"),
        P("tensor"),
        P("tensor", None),
    )
    return jax.shard_map(
        per_device,
        mesh=mesh,
        in_specs=placed,
        out_specs=(
            P("dp", None, None),
            P("dp", None, None),
            P(),
            P(None, "tensor"),
            P(None, "tensor"),
            P(),
            P(None, "tensor"),
            P(None, "tensor"),
            P("tensor"),
            P(),
            P(),
            P("tensor"),
            P("tensor"),
            P("tensor"),
            P("tensor"),
            P("tensor", None),
        ),
        check_vma=False,
    )
```

```python
import functools

import jax
import jax.numpy as jnp
from jax import lax
from jax.experimental import pallas as pl
from jax.experimental.pallas import tpu as pltpu
from jax.sharding import PartitionSpec as P

Q = 256
LANES = 128
HEAD = 8
epsilon = 1e-05
highest = lax.Precision.HIGHEST
f32 = jnp.float32
bf16 = jnp.bfloat16
NN = ((1,), (0,))
NT = ((1,), (1,))
TN = ((0,), (0,))


def mm(a, b, dims=NN):
    return lax.dot_general(
        a.astype(bf16), b.astype(bf16), (dims, ((), ())), preferred_element_type=f32
    )


def exact(a, b, dims=NN):
    return lax.dot_general(a, b, (dims, ((), ())), precision=highest, preferred_element_type=f32)


def iota(shape, dim):
    return lax.broadcasted_iota(jnp.int32, shape, dim)


def spread_matrix(width, head_dim):
    return (iota((LANES, width), 1) // head_dim == iota((LANES, width), 0)).astype(f32)


def spread_rows(width, head_dim):
    return (iota((width, LANES), 0) // head_dim == iota((width, LANES), 1)).astype(f32)


def shifted(pad_ref, start, kernel_ref, bias_ref):
    taps = kernel_ref.shape[0]
    total = bias_ref + jnp.zeros((Q, pad_ref.shape[1]), f32)
    for j in range(taps):
        total = total + kernel_ref[j : j + 1, :] * pad_ref[pl.ds(HEAD + start - taps + 1 + j, Q), :]
    return total


def softplus(v):
    return jnp.maximum(v, 0.0) + jnp.log1p(jnp.exp(-jnp.abs(v)))


def decays(dt_rows, hp_ref):
    pre = dt_rows + hp_ref[0:1, :]
    step = softplus(pre)
    rate = jnp.exp(hp_ref[1:2, :])
    log_decay = -step * rate
    lower = (iota((Q, Q), 0) >= iota((Q, Q), 1)).astype(f32)
    return pre, step, rate, log_decay, exact(lower, log_decay)


def hp_skip_col(hp):
    wide = jnp.where(iota((LANES, LANES), 0) == iota((LANES, LANES), 1), hp[2:3, :], 0.0)
    return jnp.sum(wide, axis=1, keepdims=True)


def put_rows(ref, start, value):
    count = value.shape[1] // LANES
    for r in range(value.shape[0]):
        for k in range(count):
            at = start + r * count + k
            ref[at : at + 1, :] = value[r : r + 1, k * LANES : (k + 1) * LANES]
    return start + value.shape[0] * count


def get_row(ref, at, width):
    count = width // LANES
    return jnp.concatenate([ref[at + k : at + k + 1, :] for k in range(count)], axis=1)


class Scratch:
    def __init__(self):
        self.names, self.shapes = [], []

    def add(self, name, shape):
        self.names.append(name)
        self.shapes.append(shape)

    def vmem(self, name, shape, dtype=f32):
        self.add(name, pltpu.VMEM(shape, dtype))

    def dma(self, name, count):
        self.add(name, pltpu.SemaphoreType.DMA((count,)))

    def bind(self, refs):
        return dict(zip(self.names, refs))


def remote(src, dst, send, recv, k, peer):
    return pltpu.make_async_remote_copy(
        src_ref=src,
        dst_ref=dst,
        send_sem=send.at[k],
        recv_sem=recv.at[k],
        device_id=peer,
        device_id_type=pl.DeviceIdType.MESH,
    )


def rows_of(ref, start, rows, unit):
    if not isinstance(start, int):
        start = pl.multiple_of(start, unit)
    return ref.at[pl.ds(start, rows), :]


def add_to(target, a, b):
    target[...] = (a[...].astype(f32) + b[...].astype(f32)).astype(target.dtype)


class Place:
    def __init__(self):
        n = lax.axis_size("dp") // 2
        me = lax.axis_index("dp")
        self.n = n
        self.side = lax.rem(me, 2)
        pos = me // 2
        self.pair = {"dp": me + 1 - 2 * self.side}
        self.high = (pos >= n // 2).astype(jnp.int32)
        step = 2 * (1 - 2 * self.high)
        self.inner = {"dp": me + step}
        self.outer = {"dp": me - step}
        self.end = (pos == 0) | (pos == n - 1)
        self.mid = (pos == n // 2 - 1) | (pos == n // 2)
        self.has_outer = jnp.logical_not(self.end)
        self.below = jnp.logical_not(self.mid)


class PairFirst:
    copies = 5

    def __init__(self, sc, name, rows, lanes, dtype):
        self.name, self.rows = name, rows
        half = rows // 2
        self.unit = 32 // jnp.dtype(dtype).itemsize
        assert half % self.unit == 0
        for k in ("y", "acc", "in", "mid"):
            sc.vmem(name + k, (half, lanes), dtype)
        sc.dma(name + "s", self.copies)
        sc.dma(name + "r", self.copies)

    def run(self, s, at, src, out):
        half = self.rows // 2
        y, acc, slot, mid = (s[self.name + k] for k in ("y", "acc", "in", "mid"))
        send, recv = s[self.name + "s"], s[self.name + "r"]
        keep, give = at.side * half, (1 - at.side) * half
        mine = rows_of(src, keep, half, self.unit)
        done = rows_of(out, keep, half, self.unit)
        c_y = remote(rows_of(src, give, half, self.unit), y, send, recv, 0, at.pair)
        c_in = remote(acc, slot, send, recv, 1, at.inner)
        c_mid = remote(acc, mid, send, recv, 2, at.inner)
        c_out = remote(done, done, send, recv, 3, at.outer)
        c_back = remote(done, done, send, recv, 4, at.pair)
        c_y.start()
        yield
        c_y.wait()
        add_to(acc, mine, y)

        @pl.when(at.end & at.below)
        def _():
            c_in.start()

        yield

        @pl.when(at.has_outer)
        def _():
            c_in.wait_recv()
            add_to(acc, acc, slot)

        if at.n > 4:

            @pl.when(at.has_outer & at.below)
            def _():
                c_in.start()

        @pl.when(at.mid)
        def _():
            c_mid.start()

        yield

        @pl.when(at.mid)
        def _():
            c_mid.wait()
            add_to(done, acc, mid)
            c_back.start()

        @pl.when(at.mid & at.has_outer)
        def _():
            c_out.start()

        yield

        @pl.when(at.below)
        def _():
            c_in.wait_send()
            c_out.wait_recv()
            c_back.start()

        if at.n > 4:

            @pl.when(at.below & at.has_outer)
            def _():
                c_out.start()

        yield
        c_back.wait()

        @pl.when(at.has_outer)
        def _():
            c_out.wait_send()


class LineFirst:
    copies = 6

    def __init__(self, sc, name, rows, lanes, dtype):
        self.name, self.rows = name, rows
        half = rows // 2
        self.unit = 32 // jnp.dtype(dtype).itemsize
        assert half % self.unit == 0
        for k in ("acc", "in"):
            sc.vmem(name + k, (rows, lanes), dtype)
        for k in ("mid", "y"):
            sc.vmem(name + k, (half, lanes), dtype)
        sc.dma(name + "s", self.copies)
        sc.dma(name + "r", self.copies)

    def run(self, s, at, src, out):
        half = self.rows // 2
        acc, slot, mid, y = (s[self.name + k] for k in ("acc", "in", "mid", "y"))
        send, recv = s[self.name + "s"], s[self.name + "r"]
        own, other = at.high * half, (1 - at.high) * half
        acc_own = rows_of(acc, own, half, self.unit)
        acc_other = rows_of(acc, other, half, self.unit)
        out_own = rows_of(out, own, half, self.unit)
        out_other = rows_of(out, other, half, self.unit)
        c_end = remote(src, slot, send, recv, 0, at.inner)
        c_in = remote(acc, slot, send, recv, 0, at.inner)
        c_mid = remote(acc_other, mid, send, recv, 1, at.inner)
        c_y = remote(acc_own, y, send, recv, 2, at.pair)
        c_out = remote(out_own, out_own, send, recv, 3, at.outer)
        c_back = remote(out_own, out_own, send, recv, 4, at.inner)
        c_out2 = remote(out_other, out_other, send, recv, 5, at.outer)
        if at.n == 2:
            acc[...] = src[...]
        else:

            @pl.when(at.end)
            def _():
                c_end.start()

        yield

        @pl.when(at.has_outer)
        def _():
            c_in.wait_recv()
            add_to(acc, src, slot)

        if at.n > 4:

            @pl.when(at.has_outer & at.below)
            def _():
                c_in.start()

        @pl.when(at.mid)
        def _():
            c_mid.start()

        yield

        @pl.when(at.mid)
        def _():
            c_mid.wait()
            add_to(acc_own, acc_own, mid)
            c_y.start()

        yield

        @pl.when(at.mid)
        def _():
            c_y.wait()
            add_to(out_own, acc_own, y)
            c_back.start()

        @pl.when(at.mid & at.has_outer)
        def _():
            c_out.start()

        yield

        @pl.when(at.mid)
        def _():
            c_back.wait_recv()

        @pl.when(at.mid & at.has_outer)
        def _():
            c_out2.start()

        yield

        @pl.when(at.below)
        def _():
            c_in.wait_send()
            c_out.wait_recv()

        if at.n > 4:

            @pl.when(at.below & at.has_outer)
            def _():
                c_out.start()

        @pl.when(at.below)
        def _():
            c_out2.wait_recv()

        if at.n > 4:

            @pl.when(at.below & at.has_outer)
            def _():
                c_out2.start()

        @pl.when(at.mid)
        def _():
            c_back.wait_send()

        @pl.when(at.has_outer)
        def _():
            c_out.wait_send()
            c_out2.wait_send()


def flip(axis, bit):
    me = lax.axis_index(axis)
    side = lax.rem(me // bit, 2)
    return side, {axis: me + bit - 2 * bit * side}


class Halves:
    def __init__(self, sc, name, rows, lanes, dtype, bits):
        self.name, self.rows, self.bits = name, rows, bits
        half = rows // 2
        self.unit = 32 // jnp.dtype(dtype).itemsize
        assert half % self.unit == 0
        for k in range(len(bits)):
            sc.vmem(f"{name}slot{k}", (half, lanes), dtype)
        for k in range(len(bits) - 1):
            sc.vmem(f"{name}acc{k}", (half, lanes), dtype)
        sc.dma(name + "s", len(bits) + 1)
        sc.dma(name + "r", len(bits) + 1)

    def run(self, s, at, src, out):
        half, last = self.rows // 2, len(self.bits) - 1
        send, recv = s[self.name + "s"], s[self.name + "r"]
        side, peer = flip(*self.bits[0])
        keep, give = side * half, (1 - side) * half
        done = rows_of(out, keep, half, self.unit)
        mine = rows_of(src, keep, half, self.unit)
        copy = remote(
            rows_of(src, give, half, self.unit), s[f"{self.name}slot0"], send, recv, 0, peer
        )
        copy.start()
        for k in range(last + 1):
            yield
            copy.wait()
            target = done if k == last else s[f"{self.name}acc{k}"]
            add_to(target, mine, s[f"{self.name}slot{k}"])
            if k < last:
                mine = target
                copy = remote(
                    mine, s[f"{self.name}slot{k + 1}"], send, recv, k + 1, flip(*self.bits[k + 1])[1]
                )
            else:
                copy = remote(done, done, send, recv, last + 1, peer)
            copy.start()
        yield
        copy.wait()


class Nested:
    def __init__(self, sc, name, rows, lanes, dtype, bits, inner):
        self.name, self.bits = name, bits
        self.unit = 32 // jnp.dtype(dtype).itemsize
        self.sizes = [rows >> k for k in range(len(bits) + 1)]
        for k in range(len(bits)):
            sc.vmem(f"{name}slot{k}", (self.sizes[k + 1], lanes), dtype)
            sc.vmem(f"{name}acc{k}", (self.sizes[k + 1], lanes), dtype)
        sc.dma(name + "s", 2 * len(bits))
        sc.dma(name + "r", 2 * len(bits))
        self.inner = inner(sc, name + "i", self.sizes[-1], lanes, dtype)

    def run(self, s, at, src, out):
        send, recv = s[self.name + "s"], s[self.name + "r"]
        off, trail, ref = 0, [], src
        for k, bit in enumerate(self.bits):
            half = self.sizes[k + 1]
            side, peer = flip(*bit)
            keep, give = side * half, (1 - side) * half
            slot, acc = s[f"{self.name}slot{k}"], s[f"{self.name}acc{k}"]
            copy = remote(rows_of(ref, give, half, self.unit), slot, send, recv, k, peer)
            copy.start()
            yield
            copy.wait()
            add_to(acc, rows_of(ref, keep, half, self.unit), slot)
            trail.append((off, peer))
            off, ref = off + keep, acc
        yield from self.inner.run(s, at, ref, rows_of(out, off, self.sizes[-1], self.unit))
        count = len(self.bits)
        for k in reversed(range(count)):
            parent, peer = trail[k]
            part = rows_of(out, off, self.sizes[k + 1], self.unit)
            copy = remote(part, part, send, recv, count + k, peer)
            copy.start()
            yield
            copy.wait()
            off = parent


class Small:
    def __init__(self, sc, name, rows, lanes, extra, bits):
        self.name, self.rows, self.extra, self.bits = name, rows, extra, bits
        for k in range(len(bits)):
            sc.vmem(f"{name}slot{k}", (extra, lanes), f32)
            sc.vmem(f"{name}acc{k}", (extra, lanes), f32)
        sc.dma(name + "s", len(bits))
        sc.dma(name + "r", len(bits))
        self.inner = PairFirst(sc, name + "i", rows + extra, lanes, f32)

    def run(self, s, at, src, out):
        send, recv = s[self.name + "s"], s[self.name + "r"]
        tail = src.at[pl.ds(self.rows, self.extra), :]
        ref = tail
        for k, bit in enumerate(self.bits):
            slot, acc = s[f"{self.name}slot{k}"], s[f"{self.name}acc{k}"]
            copy = remote(ref, slot, send, recv, k, flip(*bit)[1])
            copy.start()
            yield
            copy.wait()
            add_to(acc, ref, slot)
            ref = acc
        tail[...] = ref[...]
        yield from self.inner.run(s, at, src, out)


def greet(at, bits):
    barrier = pltpu.get_barrier_semaphore()

    def hello(peer):
        pl.semaphore_signal(
            barrier, inc=1, device_id=peer, device_id_type=pl.DeviceIdType.MESH
        )

    size = lax.axis_size("tensor")
    me = lax.axis_index("tensor")
    for d in range(1, size):
        hello({"tensor": lax.rem(me + d, size)})
    hello(at.pair)
    hello(at.inner)

    @pl.when(at.has_outer)
    def _():
        hello(at.outer)

    def meet():
        pl.semaphore_wait(barrier, size + 1 + at.has_outer.astype(jnp.int32))

    return meet


def exchange(s, c, stats):
    size = lax.axis_size("tensor")
    me = lax.axis_index("tensor")
    copies = []
    for d in range(1, size):
        k = c * (size - 1) + d - 1
        copy = remote(
            stats.at[c], s["st_slot"].at[k], s["st_s"], s["st_r"], k, {"tensor": lax.rem(me + d, size)}
        )
        copy.start()
        copies.append((copy, k))
    return copies


def front(heads, a, s, ready, meet):
    length, inner = s["mixed"].shape
    states = a["cbc"].shape[1] // 2
    head_dim = inner // heads
    per = LANES // head_dim
    chunks = length // Q
    hp, x_o, bc_o, state_o = s["hp"], s["x"], s["bc"], s["state"]
    wdt_s = s["wdt"]
    spread = spread_matrix(inner, head_dim)
    x_o[0:HEAD, :] = jnp.zeros((HEAD, inner), f32)
    bc_o[0:HEAD, :] = jnp.zeros((HEAD, 2 * states), f32)
    hp[...] = jnp.zeros(hp.shape, f32)
    wdt_s[...] = jnp.zeros(wdt_s.shape, bf16)
    causal = iota((Q, Q), 0) >= iota((Q, Q), 1)
    lane = iota((Q, LANES), 1)
    ready("tok", "ng")
    for c in range(chunks):
        rows = pl.ds(c * Q, Q)
        t = a["tok"][rows, :].astype(f32)
        n = t * lax.rsqrt(jnp.mean(t * t, axis=-1, keepdims=True) + epsilon) * row(a["ng"])
        s["normed"][rows, :] = n.astype(bf16)
    ready("dtw", "dtb", "alog", "dskip", "wbc")
    wdt_s[0:heads, :] = a["dtw"][...]
    for k, name in enumerate(("dtb", "alog", "dskip")):
        hp[k : k + 1, 0:heads] = row(a[name])
    for c in range(chunks):
        rows = pl.ds(c * Q, Q)
        n = s["normed"][rows, :]
        bc_o[pl.ds(HEAD + c * Q, Q), :] = mm(n, a["wbc"][...])
        s["dt"][rows, :] = mm(n, wdt_s[...], NT)
    ready("wx")
    for c in range(chunks):
        x_o[pl.ds(HEAD + c * Q, Q), :] = mm(s["normed"][pl.ds(c * Q, Q), :], a["wx"][...])
    ready("wz", "wo", "cot")
    for c in range(chunks):
        rows = pl.ds(c * Q, Q)
        s["gate"][rows, :] = mm(s["normed"][rows, :], a["wz"][...])
        s["dgn"][rows, :] = mm(a["cot"][rows, :], a["wo"][...], NT)
    ready("cx", "cxb", "cbc", "cbcb", "gg")
    copies = []
    for c in range(chunks):
        rows = pl.ds(c * Q, Q)
        v = shifted(x_o, c * Q, a["cx"], row(a["cxb"]))
        xc = v * jax.nn.sigmoid(v)
        v = shifted(bc_o, c * Q, a["cbc"], row(a["cbcb"]))
        bcc = v * jax.nn.sigmoid(v)
        b = bcc[:, :states].astype(bf16)
        cc = bcc[:, states:].astype(bf16)
        _, step, _, _, cum = decays(s["dt"][rows, :], hp)
        s["cum"][rows, :] = cum
        cum_t = jnp.transpose(cum)
        u = xc * exact(step, spread)
        scores = mm(cc, b, NT)
        outs = []
        for g in range(inner // LANES):
            part = u[:, g * LANES : (g + 1) * LANES]
            acc = jnp.zeros((Q, LANES), f32)
            for k in range(per):
                h = g * per + k
                e = jnp.exp(jnp.where(causal, cum[:, h : h + 1] - cum_t[h : h + 1, :], -1e30))
                acc = acc + mm(scores * e, jnp.where(lane // head_dim == k, part, 0.0))
            outs.append(acc)
        mixed = jnp.concatenate(outs, axis=1)
        if c > 0:
            mixed = mixed + mm(cc, state_o[c], NT) * exact(jnp.exp(cum), spread)
        if c + 1 < chunks:
            last = cum[Q - 1 : Q, :]
            tail = u * exact(jnp.exp(last - cum), spread)
            update = mm(tail, b, TN)
            if c > 0:
                rowdec = jnp.sum(
                    spread_rows(inner, head_dim) * jnp.exp(last), axis=1, keepdims=True
                )
                update = update + state_o[c] * rowdec
            state_o[c + 1] = update
        skip = jnp.sum(spread * hp_skip_col(hp), axis=0, keepdims=True)
        mixed = mixed + skip * xc
        s["mixed"][rows, :] = mixed
        gate = s["gate"][rows, :]
        gated = mixed * (gate * jax.nn.sigmoid(gate))
        sq = jnp.sum(gated * gated, axis=1, keepdims=True)
        pr = jnp.sum(row(a["gg"]) * s["dgn"][rows, :] * gated, axis=1, keepdims=True)
        both = jnp.where(lane == 0, sq, jnp.where(lane == 1, pr, 0.0))
        s["stats"][c] = jnp.transpose(both)[0:8, :]
        if c == 0:
            meet()
        copies.append(exchange(s, c, s["stats"]))
    return copies


def row(ref):
    return ref[...][None, :]


def back(heads, inner_total, a, s, copies, launch, hook):
    length, inner = s["mixed"].shape
    states = a["cbc"].shape[1] // 2
    head_dim = inner // heads
    per = LANES // head_dim
    taps = a["cx"].shape[0]
    chunks = length // Q
    hp, wdt_s = s["hp"], s["wdt"]
    x_r, bc_r = s["x"], s["bc"]
    gn_s, dz_s, dx_s, dbc_s, ddt_s = s["gn"], s["dz"], s["dx"], s["dbc"], s["ddt"]
    dvx_s, dvbc_s = s["dvx"], s["dvbc"]
    cx, cbc = a["cx"], a["cbc"]
    gg = row(a["gg"])
    spread = spread_matrix(inner, head_dim)
    spread_r = spread_rows(inner, head_dim)
    causal = iota((Q, Q), 0) >= iota((Q, Q), 1)
    lower = causal.astype(f32)
    lane = iota((Q, LANES), 1)
    skip = jnp.sum(spread * hp_skip_col(hp), axis=0, keepdims=True)
    dvx_s[pl.ds(length, HEAD), :] = jnp.zeros((HEAD, inner), f32)
    dvbc_s[pl.ds(length, HEAD), :] = jnp.zeros((HEAD, 2 * states), f32)
    g_gain = jnp.zeros((1, inner), f32)
    for c in range(chunks):
        rows = pl.ds(c * Q, Q)
        total = s["stats"][c]
        for copy, k in copies[c]:
            copy.wait()
            total = total + s["st_slot"][k]
        block = jnp.concatenate([total, jnp.zeros((LANES - 8, Q), f32)], axis=0)
        turned = jnp.transpose(block)
        gate = s["gate"][rows, :]
        mixed = s["mixed"][rows, :]
        sg = jax.nn.sigmoid(gate)
        act = gate * sg
        gated = mixed * act
        inv = lax.rsqrt(turned[:, 0:1] / inner_total + epsilon)
        pm = turned[:, 1:2] / inner_total
        dgn = s["dgn"][rows, :]
        normal = gated * inv
        gn_s[rows, :] = (normal * gg).astype(bf16)
        g_gain = g_gain + jnp.sum(dgn * normal, axis=0, keepdims=True)
        dg = inv * (gg * dgn) - gated * (inv * inv * inv) * pm
        s["dy"][rows, :] = dg * act
        dz_s[rows, :] = (dg * mixed * (sg * (1.0 + gate * (1.0 - sg)))).astype(bf16)
    s["p_gwo"][...] = mm(gn_s[...], a["cot"][...], TN).astype(bf16)
    launch("gwo")
    s["p_gz"][...] = mm(s["normed"][...], dz_s[...], TN).astype(bf16)
    launch("gz")
    s["p_res"][...] = mm(gn_s[...], a["wo"][...]).astype(bf16)
    launch("res")

    g_skip = jnp.zeros((1, inner), f32)
    g_alog = jnp.zeros((1, LANES), f32)
    g_dtb = jnp.zeros((1, LANES), f32)
    g_cx = [jnp.zeros((1, inner), f32) for _ in range(taps)]
    g_cxb = jnp.zeros((1, inner), f32)
    g_cbc = [jnp.zeros((1, 2 * states), f32) for _ in range(taps)]
    g_cbcb = jnp.zeros((1, 2 * states), f32)
    d_state = None
    for c in reversed(range(chunks)):
        rows = pl.ds(c * Q, Q)
        dy = s["dy"][rows, :]
        vx = shifted(x_r, c * Q, cx, row(a["cxb"]))
        sx = jax.nn.sigmoid(vx)
        xc = vx * sx
        vb = shifted(bc_r, c * Q, cbc, row(a["cbcb"]))
        sb = jax.nn.sigmoid(vb)
        bcc = vb * sb
        b = bcc[:, :states].astype(bf16)
        cc = bcc[:, states:].astype(bf16)
        pre = s["dt"][rows, :] + hp[0:1, :]
        step = softplus(pre)
        rate = jnp.exp(hp[1:2, :])
        log_decay = -step * rate
        cum = s["cum"][rows, :]
        cum_t = jnp.transpose(cum)
        stepw = exact(step, spread)
        u = xc * stepw
        scores = mm(cc, b, NT)
        d_scores = jnp.zeros((Q, Q), f32)
        d_cum = jnp.zeros((Q, LANES), f32)
        cols = jnp.zeros((8, Q), f32)
        dus = []
        for g in range(inner // LANES):
            up = u[:, g * LANES : (g + 1) * LANES].astype(bf16)
            dyp = dy[:, g * LANES : (g + 1) * LANES]
            acc = jnp.zeros((Q, LANES), f32)
            for k in range(per):
                h = g * per + k
                e = jnp.exp(jnp.where(causal, cum[:, h : h + 1] - cum_t[h : h + 1, :], -1e30))
                p = scores * e
                dyh = jnp.where(lane // head_dim == k, dyp, 0.0).astype(bf16)
                dp = mm(dyh, up, NT)
                d_scores = d_scores + dp * e
                gp = dp * p
                d_cum = d_cum + jnp.where(lane == h, jnp.sum(gp, axis=1, keepdims=True), 0.0)
                cols = cols + jnp.where(
                    iota((8, Q), 0) == h, jnp.sum(gp, axis=0, keepdims=True), 0.0
                )
                acc = acc + mm(p, dyh, TN)
                hook()
            dus.append(acc)
        du = jnp.concatenate(dus, axis=1)
        d_cum = d_cum - jnp.transpose(
            jnp.concatenate([cols, jnp.zeros((LANES - 8, Q), f32)], axis=0)
        )
        d_c = mm(d_scores, b)
        d_b = mm(d_scores, cc, TN)
        d_prev = None
        if c > 0:
            state = s["state"][c]
            decayed = exact(jnp.exp(cum), spread)
            dz = dy * decayed
            carried = mm(cc, state, NT) * dz
            d_cum = d_cum + exact(carried, spread, NT)
            d_c = d_c + mm(dz, state)
            d_prev = mm(dz, cc, TN)
        if d_state is not None:
            last = cum[Q - 1 : Q, :]
            tailw = exact(jnp.exp(last - cum), spread)
            ut = u * tailw
            dut = mm(b, d_state, NT)
            d_b = d_b + mm(ut, d_state)
            du = du + dut * tailw
            q = exact(dut * ut, spread, NT)
            d_last = jnp.sum(q, axis=0, keepdims=True)
            if c > 0:
                rowdec = jnp.sum(spread_r * jnp.exp(last), axis=1, keepdims=True)
                r = jnp.sum(d_state * s["state"][c], axis=1, keepdims=True) * rowdec
                d_last = d_last + jnp.sum(spread_r * r, axis=0, keepdims=True)
                d_prev = d_prev + d_state * rowdec
            d_cum = d_cum - q + jnp.where(iota((Q, LANES), 0) == Q - 1, d_last, 0.0)
        d_state = d_prev
        d_log = exact(lower, d_cum, TN)
        g_alog = g_alog + jnp.sum(d_log * log_decay, axis=0, keepdims=True)
        d_step = exact(du * xc, spread, NT) - d_log * rate
        d_pre = d_step * jax.nn.sigmoid(pre)
        d_pre = jnp.where(lane < heads, d_pre, 0.0)
        g_dtb = g_dtb + jnp.sum(d_pre, axis=0, keepdims=True)
        g_skip = g_skip + jnp.sum(dy * xc, axis=0, keepdims=True)
        dxc = du * stepw + skip * dy
        dvx = dxc * (sx * (1.0 + vx * (1.0 - sx)))
        dvb = jnp.concatenate([d_b, d_c], axis=1) * (sb * (1.0 + vb * (1.0 - sb)))
        dvx_s[rows, :] = dvx
        dvbc_s[rows, :] = dvb
        g_cxb = g_cxb + jnp.sum(dvx, axis=0, keepdims=True)
        g_cbcb = g_cbcb + jnp.sum(dvb, axis=0, keepdims=True)
        dx = jnp.zeros((Q, inner), f32)
        dbc = jnp.zeros((Q, 2 * states), f32)
        for j in range(taps):
            behind = pl.ds(c * Q + taps - 1 - j, Q)
            ahead = pl.ds(HEAD + c * Q - taps + 1 + j, Q)
            dx = dx + cx[j : j + 1, :] * dvx_s[behind, :]
            dbc = dbc + cbc[j : j + 1, :] * dvbc_s[behind, :]
            g_cx[j] = g_cx[j] + jnp.sum(dvx * x_r[ahead, :], axis=0, keepdims=True)
            g_cbc[j] = g_cbc[j] + jnp.sum(dvb * bc_r[ahead, :], axis=0, keepdims=True)
        dx_s[rows, :] = dx.astype(bf16)
        dbc_s[rows, :] = dbc.astype(bf16)
        ddt_s[rows, :] = d_pre.astype(bf16)
        hook()

    normed = s["normed"]
    s["p_gbc"][...] = mm(normed[...], dbc_s[...], TN).astype(bf16)
    launch("gbc")
    s["p_gx"][...] = mm(normed[...], dx_s[...], TN).astype(bf16)
    launch("gx")
    hook()
    g_ng = jnp.zeros((1, normed.shape[1]), f32)
    for c in range(chunks):
        rows = pl.ds(c * Q, Q)
        dn = mm(dz_s[rows, :], a["wz"][...], NT) + mm(dx_s[rows, :], a["wx"][...], NT)
        dn = dn + mm(dbc_s[rows, :], a["wbc"][...], NT) + mm(ddt_s[rows, :], wdt_s[...])
        s["p_dn"][rows, :] = dn.astype(bf16)
        t = a["tok"][rows, :].astype(f32)
        unit = t * lax.rsqrt(jnp.mean(t * t, axis=-1, keepdims=True) + epsilon)
        g_ng = g_ng + jnp.sum(dn * unit, axis=0, keepdims=True)
        if c == 0:
            hook()
    launch("dn")
    hook()
    gdt = mm(ddt_s[...], normed[...], TN)
    small = s["p_sm"]
    small[...] = jnp.zeros(small.shape, f32)
    at = put_rows(small, 0, gdt[0:heads, :])
    for value in (*g_cx, g_cxb, g_gain, g_dtb, g_alog, exact(g_skip, spread, NT)):
        at = put_rows(small, at, value)
    at = -(-at // 8) * 8
    for value in (*g_cbc, g_cbcb, g_ng):
        at = put_rows(small, at, value)
    launch("sm")


INPUTS = (
    "tok", "cot", "ng", "wz", "wx", "wbc", "dtw", "cx", "cxb", "cbc", "cbcb",
    "dtb", "alog", "dskip", "gg", "wo",
)
FETCH = (
    "tok", "ng", "dtw", "dtb", "alog", "dskip", "wbc", "wx", "wz", "wo", "cot",
    "cx", "cxb", "cbc", "cbcb", "gg",
)
RESULTS = ("res", "dn", "gz", "gx", "gwo", "gbc", "sm")


def kernel_main(heads, inner_total, sc, plan, hooks, bits, *refs):
    hbm = dict(zip(INPUTS, refs))
    outs = dict(zip(RESULTS, refs[len(INPUTS) :]))
    s = sc.bind(refs[len(INPUTS) + len(RESULTS) :])
    at = Place()
    a = {name: s["a_" + name] for name in INPUTS}
    loads = {}
    for k, name in enumerate(FETCH):
        loads[name] = pltpu.make_async_copy(hbm[name], a[name], s["loads"].at[k])
        loads[name].start()
    meet = greet(at, bits)

    def ready(*names):
        for name in names:
            loads[name].wait()

    running = []

    def launch(name):
        for stream, source, start, rows in plan:
            if source == name:
                run = stream.run(
                    s,
                    at,
                    s["p_" + name].at[pl.ds(start, rows), :],
                    s["o_" + name].at[pl.ds(start, rows), :],
                )
                next(run)
                k = len(running)
                store = pltpu.make_async_copy(
                    s["o_" + name].at[pl.ds(start, rows), :],
                    outs[name].at[pl.ds(start, rows), :],
                    s["stores"].at[k],
                )
                running.append([stream.name, run, True, store])

    def forward(entry):
        if next(entry[1], 1) is not None:
            entry[2] = False
            entry[3].start()

    def advance(name):
        for entry in running:
            if entry[2] and entry[0] == name:
                forward(entry)

    turn = iter(hooks)

    def hook():
        for name in next(turn, ()):
            advance(name)

    copies = front(heads, a, s, ready, meet)
    back(heads, inner_total, a, s, copies, launch, hook)
    for names in turn:
        for name in names:
            advance(name)
    while any(entry[2] for entry in running):
        for entry in running:
            if entry[2]:
                forward(entry)
    for entry in running:
        entry[3].wait()


SUMS = ("tok", "cot", "ng", *RESULTS)
FINAL = (
    "res", "gt", "ng", "gz", "gx", "gbc", "gdt", "cx", "cxb", "cbc", "cbcb",
    "dtb", "alog", "skip", "gain", "gwo",
)


def kernel_finish(sc, *refs):
    count = len(SUMS) + len(FINAL)
    s = sc.bind(refs[count:])
    loads = {}
    for k, name in enumerate(("gwo", "gz", "gx", "gbc", "sm", "tok", "cot", "ng", "res", "dn")):
        loads[name] = pltpu.make_async_copy(
            refs[SUMS.index(name)], s["i_" + name], s["loads"].at[k]
        )
        loads[name].start()
    stores = []

    def store(*names):
        for name in names:
            k = FINAL.index(name)
            copy = pltpu.make_async_copy(s["o_" + name], refs[len(SUMS) + k], s["stores"].at[k])
            copy.start()
            stores.append(copy)

    for name in ("gwo", "gz", "gx", "gbc"):
        loads[name].wait()
        s["o_" + name][...] = s["i_" + name][...].astype(f32)
        store(name)
    loads["sm"].wait()
    sums = s["i_sm"]
    at = 0
    for name in ("gdt", "cx"):
        out = s["o_" + name]
        for r in range(out.shape[0]):
            out[r : r + 1, :] = get_row(sums, at, out.shape[1])
            at += out.shape[1] // LANES
    for name in ("cxb", "gain"):
        out = s["o_" + name]
        out[...] = get_row(sums, at, out.shape[0])[0]
        at += out.shape[0] // LANES
    for name in ("dtb", "alog", "skip"):
        out = s["o_" + name]
        out[...] = sums[at, 0 : out.shape[0]]
        at += 1
    at = -(-at // 8) * 8
    out = s["o_cbc"]
    for r in range(out.shape[0]):
        out[r : r + 1, :] = get_row(sums, at, out.shape[1])
        at += out.shape[1] // LANES
    for name in ("cbcb", "ng"):
        out = s["o_" + name]
        out[...] = get_row(sums, at, out.shape[0])[0]
        at += out.shape[0] // LANES
    store("gdt", "cx", "cxb", "gain", "dtb", "alog", "skip", "cbc", "cbcb", "ng")
    for name in ("tok", "cot", "ng", "res", "dn"):
        loads[name].wait()
    for c in range(s["i_tok"].shape[0] // Q):
        rows = pl.ds(c * Q, Q)
        t = s["i_tok"][rows, :].astype(f32)
        s["o_res"][rows, :] = (t + s["i_res"][rows, :].astype(f32)).astype(bf16)
        r = lax.rsqrt(jnp.mean(t * t, axis=-1, keepdims=True) + epsilon)
        gd = s["i_dn"][rows, :].astype(f32) * row(s["i_ng"])
        mean = jnp.mean(t * gd, axis=-1, keepdims=True)
        d = r * gd - t * (r * r * r) * mean
        s["o_gt"][rows, :] = (s["i_cot"][rows, :].astype(f32) + d).astype(bf16)
    store("res", "gt")
    for copy in stores:
        copy.wait()


PATHS = {
    "gwo": (PairFirst, PairFirst, PairFirst, PairFirst),
    "gz": (PairFirst, PairFirst, PairFirst, PairFirst),
    "gx": (PairFirst, PairFirst, LineFirst, PairFirst, PairFirst, LineFirst),
}
HOOKS = (
    (),
    (),
    (),
    ("res", "gwo0", ),
    (),
    (),
    ("gwo1", ),
    (),
    (),
    ("gwo2", ),
    ("gwo0", ),
    (),
    ("gwo3", ),
    ("gwo1", ),
    ("gz0", ),
    ("gwo2", "gbc", "gwo0", ),
    ("gz1", "gwo3", ),
    ("gz2", "gwo1", "res", "gx2", "gz3", "dn", "sm", "gwo2", ),
    ("gwo0", "gx0", "gbc", "res", "gx5", "gx1", "gwo3", "gwo1", ),
    ("gx3", "gx2", "gz0", "gx4", "gwo2", "gx5", "gz1", "gwo0", ),
    ("gwo3", "gz2", "gz0", "gz3", "gwo1", "gz1", "gx0", "gbc", ),
    ("gwo2", "gz2", "gx1", "gz0", "dn", "sm", "gx3", "gwo3", ),
    ("gz3", "gz1", "gx4", "gx2", "gx0", "dn", "gbc", "gx5", ),
    ("gz2", "gx1", "gx3", "gz0", "gz3", "gx4", "gz1", "gx2", ),
    ("gx0", "gbc", "gz2", "sm", "gx5", "gx1", "sm", "gz3", ),
    ("gx3", "gx0", "gx4", "sm", "gx1", "gx2", "gx3", "gbc", ),
    ("gx4", "gx5", "sm", "gbc", "sm", "gbc", "gbc", ),
)


def call(body, args, outs, scratch=(), **params):
    hbm = pl.BlockSpec(memory_space=pltpu.HBM)
    return pl.pallas_call(
        body,
        out_shape=[jax.ShapeDtypeStruct(s, d) for s, d in outs],
        in_specs=[hbm] * len(args),
        out_specs=[hbm] * len(outs),
        scratch_shapes=list(scratch),
        compiler_params=pltpu.CompilerParams(vmem_limit_bytes=63 * 1024 * 1024, **params),
    )(*args)


def per_device(
    tokens, cotangent, norm_gain, w_z, w_x, w_bc, w_dt, conv_x, conv_x_bias, conv_bc,
    conv_bc_bias, dt_bias, a_log, d_skip, gate_gain, w_out,
):
    seqs, length, width = tokens.shape
    assert seqs == 1 and length % Q == 0
    heads = dt_bias.shape[0]
    inner = w_z.shape[1]
    wide = w_bc.shape[1]
    states = wide // 2
    taps = conv_x.shape[0]
    dp, tensor = lax.axis_size("dp"), lax.axis_size("tensor")
    assert dp % 4 == 0 and tensor & (tensor - 1) == 0
    inner_total = inner * tensor
    chunks = length // Q
    tok = tokens.reshape(length, width)
    cot = cotangent.reshape(length, width)
    args = (
        tok, cot, norm_gain, w_z, w_x, w_bc, w_dt.T, conv_x, conv_x_bias, conv_bc,
        conv_bc_bias, dt_bias, a_log, d_skip, gate_gain, w_out,
    )
    bits = [("tensor", 1 << k) for k in range(tensor.bit_length() - 1)]
    sc = Scratch()
    for name, value in zip(INPUTS, args):
        sc.vmem("a_" + name, value.shape, value.dtype)
    sc.dma("loads", len(INPUTS))
    sc.vmem("wdt", (LANES, width), bf16)
    sc.vmem("hp", (8, LANES))
    sc.vmem("normed", (length, width), bf16)
    for name in ("gate", "mixed", "dgn", "dy"):
        sc.vmem(name, (length, inner))
    for name in ("x", "dvx"):
        sc.vmem(name, (length + HEAD, inner))
    for name in ("bc", "dvbc"):
        sc.vmem(name, (length + HEAD, wide))
    for name in ("dt", "cum"):
        sc.vmem(name, (length, LANES))
    sc.vmem("state", (chunks, inner, states))
    sc.vmem("stats", (chunks, 8, Q))
    sc.vmem("st_slot", (chunks * (tensor - 1), 8, Q))
    sc.dma("st_s", chunks * (tensor - 1))
    sc.dma("st_r", chunks * (tensor - 1))
    for name in ("gn", "dz", "dx"):
        sc.vmem(name, (length, inner), bf16)
    sc.vmem("dbc", (length, wide), bf16)
    sc.vmem("ddt", (length, LANES), bf16)
    own_rows = heads * width // LANES + (taps + 2) * inner // LANES + 3
    own_rows = -(-own_rows // 8) * 8
    all_rows = (taps + 1) * wide // LANES + width // LANES
    all_rows = -(-(own_rows + all_rows) // 16) * 16 - own_rows
    results = [
        ((length, width), bf16),
        ((length, width), bf16),
        ((width, inner), bf16),
        ((width, inner), bf16),
        ((inner, width), bf16),
        ((width, wide), bf16),
        ((own_rows + all_rows, LANES), f32),
    ]
    for name, (shape, dtype) in zip(RESULTS, results):
        sc.vmem("p_" + name, shape, dtype)
        sc.vmem("o_" + name, shape, dtype)
    plan = []

    def split(name, kinds):
        shape, dtype = results[RESULTS.index(name)]
        rows = shape[0] // len(kinds)
        for k, kind in enumerate(kinds):
            plan.append((kind(sc, f"{name}{k}", rows, shape[1], dtype), name, k * rows, rows))

    split("gwo", PATHS["gwo"])
    split("gz", PATHS["gz"])
    split("gx", PATHS["gx"])
    for name in ("res", "dn"):
        shape, dtype = results[RESULTS.index(name)]
        plan.append((Halves(sc, name, *shape, dtype, bits), name, 0, shape[0]))
    plan.append((Nested(sc, "gbc", width, wide, bf16, bits, PairFirst), "gbc", 0, width))
    plan.append((Small(sc, "sm", own_rows, LANES, all_rows, bits), "sm", 0, own_rows + all_rows))
    sc.dma("stores", len(plan))
    sums = call(
        functools.partial(kernel_main, heads, inner_total, sc, plan, HOOKS, bits),
        args,
        results,
        sc.shapes,
        collective_id=0,
        has_side_effects=True,
    )
    final = [
        ((length, width), bf16),
        ((length, width), bf16),
        ((width,), f32),
        ((width, inner), f32),
        ((width, inner), f32),
        ((width, wide), f32),
        ((heads, width), f32),
        ((taps, inner), f32),
        ((inner,), f32),
        ((taps, wide), f32),
        ((wide,), f32),
        ((heads,), f32),
        ((heads,), f32),
        ((heads,), f32),
        ((inner,), f32),
        ((inner, width), f32),
    ]
    last = Scratch()
    sources = (tok, cot, norm_gain, *sums)
    for name, value in zip(SUMS, sources):
        last.vmem("i_" + name, value.shape, value.dtype)
    for name, (shape, dtype) in zip(FINAL, final):
        last.vmem("o_" + name, shape, dtype)
    last.dma("loads", len(SUMS))
    last.dma("stores", len(FINAL))
    outs = call(functools.partial(kernel_finish, last), sources, final, last.shapes)
    outs = list(outs)
    for k in range(2):
        outs[k] = outs[k].reshape(seqs, length, width)
    outs[6] = outs[6].T
    return tuple(outs)


def solution(mesh):
    placed = (
        P("dp", None, None),
        P("dp", None, None),
        P(),
        P(None, "tensor"),
        P(None, "tensor"),
        P(),
        P(None, "tensor"),
        P(None, "tensor"),
        P("tensor"),
        P(),
        P(),
        P("tensor"),
        P("tensor"),
        P("tensor"),
        P("tensor"),
        P("tensor", None),
    )
    return jax.shard_map(
        per_device,
        mesh=mesh,
        in_specs=placed,
        out_specs=(
            P("dp", None, None),
            P("dp", None, None),
            P(),
            P(None, "tensor"),
            P(None, "tensor"),
            P(),
            P(None, "tensor"),
            P(None, "tensor"),
            P("tensor"),
            P(),
            P(),
            P("tensor"),
            P("tensor"),
            P("tensor"),
            P("tensor"),
            P("tensor", None),
        ),
        check_vma=False,
    )
```

```python
import functools

import jax
import jax.numpy as jnp
from jax import lax
from jax.experimental import pallas as pl
from jax.experimental.pallas import tpu as pltpu
from jax.sharding import PartitionSpec as P

Q = 256
LANES = 128
HEAD = 8
epsilon = 1e-05
highest = lax.Precision.HIGHEST
f32 = jnp.float32
bf16 = jnp.bfloat16
NN = ((1,), (0,))
NT = ((1,), (1,))
TN = ((0,), (0,))


def mm(a, b, dims=NN):
    return lax.dot_general(
        a.astype(bf16), b.astype(bf16), (dims, ((), ())), preferred_element_type=f32
    )


def exact(a, b, dims=NN):
    return lax.dot_general(a, b, (dims, ((), ())), precision=highest, preferred_element_type=f32)


def iota(shape, dim):
    return lax.broadcasted_iota(jnp.int32, shape, dim)


def spread_matrix(width, head_dim):
    return (iota((LANES, width), 1) // head_dim == iota((LANES, width), 0)).astype(f32)


def spread_rows(width, head_dim):
    return (iota((width, LANES), 0) // head_dim == iota((width, LANES), 1)).astype(f32)


def shifted(pad_ref, start, kernel_ref, bias_ref):
    taps = kernel_ref.shape[0]
    total = bias_ref + jnp.zeros((Q, pad_ref.shape[1]), f32)
    for j in range(taps):
        total = total + kernel_ref[j : j + 1, :] * pad_ref[pl.ds(HEAD + start - taps + 1 + j, Q), :]
    return total


def softplus(v):
    return jnp.maximum(v, 0.0) + jnp.log1p(jnp.exp(-jnp.abs(v)))


def decays(dt_rows, hp_ref):
    pre = dt_rows + hp_ref[0:1, :]
    step = softplus(pre)
    rate = jnp.exp(hp_ref[1:2, :])
    log_decay = -step * rate
    lower = (iota((Q, Q), 0) >= iota((Q, Q), 1)).astype(f32)
    return pre, step, rate, log_decay, exact(lower, log_decay)


def hp_skip_col(hp):
    wide = jnp.where(iota((LANES, LANES), 0) == iota((LANES, LANES), 1), hp[2:3, :], 0.0)
    return jnp.sum(wide, axis=1, keepdims=True)


def put_rows(ref, start, value):
    count = value.shape[1] // LANES
    for r in range(value.shape[0]):
        for k in range(count):
            at = start + r * count + k
            ref[at : at + 1, :] = value[r : r + 1, k * LANES : (k + 1) * LANES]
    return start + value.shape[0] * count


def get_row(ref, at, width):
    count = width // LANES
    return jnp.concatenate([ref[at + k : at + k + 1, :] for k in range(count)], axis=1)


class Refs(dict):
    __getattr__ = dict.__getitem__


class Scratch:
    def __init__(self):
        self.names, self.shapes = [], []

    def add(self, name, shape):
        self.names.append(name)
        self.shapes.append(shape)

    def vmem(self, name, shape, dtype=f32):
        self.add(name, pltpu.VMEM(shape, dtype))

    def dma(self, name, count):
        self.add(name, pltpu.SemaphoreType.DMA((count,)))

    def bind(self, refs):
        return Refs(zip(self.names, refs))


def remote(src, dst, send, recv, k, peer):
    return pltpu.make_async_remote_copy(
        src_ref=src,
        dst_ref=dst,
        send_sem=send.at[k],
        recv_sem=recv.at[k],
        device_id=peer,
        device_id_type=pl.DeviceIdType.MESH,
    )


def rows_of(ref, start, rows, unit):
    if not isinstance(start, int):
        start = pl.multiple_of(start, unit)
    return ref.at[pl.ds(start, rows), :]


def add_to(target, a, b):
    target[...] = (a[...].astype(f32) + b[...].astype(f32)).astype(target.dtype)


class Place:
    def __init__(self):
        n = lax.axis_size("dp") // 2
        me = lax.axis_index("dp")
        self.n = n
        self.side = lax.rem(me, 2)
        pos = me // 2
        self.pair = {"dp": me + 1 - 2 * self.side}
        self.high = (pos >= n // 2).astype(jnp.int32)
        step = 2 * (1 - 2 * self.high)
        self.inner = {"dp": me + step}
        self.outer = {"dp": me - step}
        self.end = (pos == 0) | (pos == n - 1)
        self.mid = (pos == n // 2 - 1) | (pos == n // 2)
        self.has_outer = jnp.logical_not(self.end)
        self.below = jnp.logical_not(self.mid)


class PairFirst:
    copies = 5

    def __init__(self, sc, name, rows, lanes, dtype):
        self.name, self.rows = name, rows
        half = rows // 2
        self.unit = 32 // jnp.dtype(dtype).itemsize
        assert half % self.unit == 0
        for k in ("y", "acc", "in", "mid"):
            sc.vmem(name + k, (half, lanes), dtype)
        sc.dma(name + "s", self.copies)
        sc.dma(name + "r", self.copies)

    def run(self, s, at, src, out):
        half = self.rows // 2
        y, acc, slot, mid = (s[self.name + k] for k in ("y", "acc", "in", "mid"))
        send, recv = s[self.name + "s"], s[self.name + "r"]
        keep, give = at.side * half, (1 - at.side) * half
        mine = rows_of(src, keep, half, self.unit)
        done = rows_of(out, keep, half, self.unit)
        c_y = remote(rows_of(src, give, half, self.unit), y, send, recv, 0, at.pair)
        c_in = remote(acc, slot, send, recv, 1, at.inner)
        c_mid = remote(acc, mid, send, recv, 2, at.inner)
        c_out = remote(done, done, send, recv, 3, at.outer)
        c_back = remote(done, done, send, recv, 4, at.pair)
        c_y.start()
        yield
        c_y.wait()
        add_to(acc, mine, y)

        @pl.when(at.end & at.below)
        def _():
            c_in.start()

        yield

        @pl.when(at.has_outer)
        def _():
            c_in.wait_recv()
            add_to(acc, acc, slot)

        if at.n > 4:

            @pl.when(at.has_outer & at.below)
            def _():
                c_in.start()

        @pl.when(at.mid)
        def _():
            c_mid.start()

        yield

        @pl.when(at.mid)
        def _():
            c_mid.wait()
            add_to(done, acc, mid)
            c_back.start()

        @pl.when(at.mid & at.has_outer)
        def _():
            c_out.start()

        yield

        @pl.when(at.below)
        def _():
            c_in.wait_send()
            c_out.wait_recv()
            c_back.start()

        if at.n > 4:

            @pl.when(at.below & at.has_outer)
            def _():
                c_out.start()

        yield
        c_back.wait()

        @pl.when(at.has_outer)
        def _():
            c_out.wait_send()


class LineFirst:
    copies = 6

    def __init__(self, sc, name, rows, lanes, dtype):
        self.name, self.rows = name, rows
        half = rows // 2
        self.unit = 32 // jnp.dtype(dtype).itemsize
        assert half % self.unit == 0
        for k in ("acc", "in"):
            sc.vmem(name + k, (rows, lanes), dtype)
        for k in ("mid", "y"):
            sc.vmem(name + k, (half, lanes), dtype)
        sc.dma(name + "s", self.copies)
        sc.dma(name + "r", self.copies)

    def run(self, s, at, src, out):
        half = self.rows // 2
        acc, slot, mid, y = (s[self.name + k] for k in ("acc", "in", "mid", "y"))
        send, recv = s[self.name + "s"], s[self.name + "r"]
        own, other = at.high * half, (1 - at.high) * half
        acc_own = rows_of(acc, own, half, self.unit)
        acc_other = rows_of(acc, other, half, self.unit)
        out_own = rows_of(out, own, half, self.unit)
        out_other = rows_of(out, other, half, self.unit)
        c_end = remote(src, slot, send, recv, 0, at.inner)
        c_in = remote(acc, slot, send, recv, 0, at.inner)
        c_mid = remote(acc_other, mid, send, recv, 1, at.inner)
        c_y = remote(acc_own, y, send, recv, 2, at.pair)
        c_out = remote(out_own, out_own, send, recv, 3, at.outer)
        c_back = remote(out_own, out_own, send, recv, 4, at.inner)
        c_out2 = remote(out_other, out_other, send, recv, 5, at.outer)
        if at.n == 2:
            acc[...] = src[...]
        else:

            @pl.when(at.end)
            def _():
                c_end.start()

        yield

        @pl.when(at.has_outer)
        def _():
            c_in.wait_recv()
            add_to(acc, src, slot)

        if at.n > 4:

            @pl.when(at.has_outer & at.below)
            def _():
                c_in.start()

        @pl.when(at.mid)
        def _():
            c_mid.start()

        yield

        @pl.when(at.mid)
        def _():
            c_mid.wait()
            add_to(acc_own, acc_own, mid)
            c_y.start()

        yield

        @pl.when(at.mid)
        def _():
            c_y.wait()
            add_to(out_own, acc_own, y)
            c_back.start()

        @pl.when(at.mid & at.has_outer)
        def _():
            c_out.start()

        yield

        @pl.when(at.mid)
        def _():
            c_back.wait_recv()

        @pl.when(at.mid & at.has_outer)
        def _():
            c_out2.start()

        yield

        @pl.when(at.below)
        def _():
            c_in.wait_send()
            c_out.wait_recv()

        if at.n > 4:

            @pl.when(at.below & at.has_outer)
            def _():
                c_out.start()

        @pl.when(at.below)
        def _():
            c_out2.wait_recv()

        if at.n > 4:

            @pl.when(at.below & at.has_outer)
            def _():
                c_out2.start()

        @pl.when(at.mid)
        def _():
            c_back.wait_send()

        @pl.when(at.has_outer)
        def _():
            c_out.wait_send()
            c_out2.wait_send()


def flip(axis, bit):
    me = lax.axis_index(axis)
    side = lax.rem(me // bit, 2)
    return side, {axis: me + bit - 2 * bit * side}


class Halves:
    def __init__(self, sc, name, rows, lanes, dtype, bits):
        self.name, self.rows, self.bits = name, rows, bits
        half = rows // 2
        self.unit = 32 // jnp.dtype(dtype).itemsize
        assert half % self.unit == 0
        for k in range(len(bits)):
            sc.vmem(f"{name}slot{k}", (half, lanes), dtype)
        for k in range(len(bits) - 1):
            sc.vmem(f"{name}acc{k}", (half, lanes), dtype)
        sc.dma(name + "s", len(bits) + 1)
        sc.dma(name + "r", len(bits) + 1)

    def run(self, s, at, src, out):
        half, last = self.rows // 2, len(self.bits) - 1
        send, recv = s[self.name + "s"], s[self.name + "r"]
        side, peer = flip(*self.bits[0])
        keep, give = side * half, (1 - side) * half
        done = rows_of(out, keep, half, self.unit)
        mine = rows_of(src, keep, half, self.unit)
        copy = remote(
            rows_of(src, give, half, self.unit), s[f"{self.name}slot0"], send, recv, 0, peer
        )
        copy.start()
        for k in range(last + 1):
            yield
            copy.wait()
            target = done if k == last else s[f"{self.name}acc{k}"]
            add_to(target, mine, s[f"{self.name}slot{k}"])
            if k < last:
                mine = target
                copy = remote(
                    mine, s[f"{self.name}slot{k + 1}"], send, recv, k + 1, flip(*self.bits[k + 1])[1]
                )
            else:
                copy = remote(done, done, send, recv, last + 1, peer)
            copy.start()
        yield
        copy.wait()


class Nested:
    def __init__(self, sc, name, rows, lanes, dtype, bits, inner):
        self.name, self.bits = name, bits
        self.unit = 32 // jnp.dtype(dtype).itemsize
        self.sizes = [rows >> k for k in range(len(bits) + 1)]
        for k in range(len(bits)):
            sc.vmem(f"{name}slot{k}", (self.sizes[k + 1], lanes), dtype)
            sc.vmem(f"{name}acc{k}", (self.sizes[k + 1], lanes), dtype)
        sc.dma(name + "s", 2 * len(bits))
        sc.dma(name + "r", 2 * len(bits))
        self.inner = inner(sc, name + "i", self.sizes[-1], lanes, dtype)

    def run(self, s, at, src, out):
        send, recv = s[self.name + "s"], s[self.name + "r"]
        off, trail, ref = 0, [], src
        for k, bit in enumerate(self.bits):
            half = self.sizes[k + 1]
            side, peer = flip(*bit)
            keep, give = side * half, (1 - side) * half
            slot, acc = s[f"{self.name}slot{k}"], s[f"{self.name}acc{k}"]
            copy = remote(rows_of(ref, give, half, self.unit), slot, send, recv, k, peer)
            copy.start()
            yield
            copy.wait()
            add_to(acc, rows_of(ref, keep, half, self.unit), slot)
            trail.append((off, peer))
            off, ref = off + keep, acc
        yield from self.inner.run(s, at, ref, rows_of(out, off, self.sizes[-1], self.unit))
        count = len(self.bits)
        for k in reversed(range(count)):
            parent, peer = trail[k]
            part = rows_of(out, off, self.sizes[k + 1], self.unit)
            copy = remote(part, part, send, recv, count + k, peer)
            copy.start()
            yield
            copy.wait()
            off = parent


class Small:
    def __init__(self, sc, name, rows, lanes, extra, bits):
        self.name, self.rows, self.extra, self.bits = name, rows, extra, bits
        for k in range(len(bits)):
            sc.vmem(f"{name}slot{k}", (extra, lanes), f32)
            sc.vmem(f"{name}acc{k}", (extra, lanes), f32)
        sc.dma(name + "s", len(bits))
        sc.dma(name + "r", len(bits))
        self.inner = PairFirst(sc, name + "i", rows + extra, lanes, f32)

    def run(self, s, at, src, out):
        send, recv = s[self.name + "s"], s[self.name + "r"]
        tail = src.at[pl.ds(self.rows, self.extra), :]
        ref = tail
        for k, bit in enumerate(self.bits):
            slot, acc = s[f"{self.name}slot{k}"], s[f"{self.name}acc{k}"]
            copy = remote(ref, slot, send, recv, k, flip(*bit)[1])
            copy.start()
            yield
            copy.wait()
            add_to(acc, ref, slot)
            ref = acc
        tail[...] = ref[...]
        yield from self.inner.run(s, at, src, out)


def greet(at, bits):
    barrier = pltpu.get_barrier_semaphore()

    def hello(peer):
        pl.semaphore_signal(
            barrier, inc=1, device_id=peer, device_id_type=pl.DeviceIdType.MESH
        )

    size = lax.axis_size("tensor")
    me = lax.axis_index("tensor")
    for d in range(1, size):
        hello({"tensor": lax.rem(me + d, size)})
    hello(at.pair)
    hello(at.inner)

    @pl.when(at.has_outer)
    def _():
        hello(at.outer)

    def meet():
        pl.semaphore_wait(barrier, size + 1 + at.has_outer.astype(jnp.int32))

    return meet


def exchange(s, c, stats):
    size = lax.axis_size("tensor")
    me = lax.axis_index("tensor")
    copies = []
    for d in range(1, size):
        k = c * (size - 1) + d - 1
        copy = remote(
            stats.at[c], s.st_slot.at[k], s.st_s, s.st_r, k, {"tensor": lax.rem(me + d, size)}
        )
        copy.start()
        copies.append((copy, k))
    return copies


def front(heads, a, s, ready, meet):
    length, inner = s.mixed.shape
    states = a.cbc.shape[1] // 2
    head_dim = inner // heads
    per = LANES // head_dim
    chunks = length // Q
    hp, x_o, bc_o, state_o = s.hp, s.x, s.bc, s.state
    wdt_s = s.wdt
    spread = spread_matrix(inner, head_dim)
    x_o[0:HEAD, :] = jnp.zeros((HEAD, inner), f32)
    bc_o[0:HEAD, :] = jnp.zeros((HEAD, 2 * states), f32)
    hp[...] = jnp.zeros(hp.shape, f32)
    wdt_s[...] = jnp.zeros(wdt_s.shape, bf16)
    causal = iota((Q, Q), 0) >= iota((Q, Q), 1)
    lane = iota((Q, LANES), 1)
    ready("tok", "ng")
    for c in range(chunks):
        rows = pl.ds(c * Q, Q)
        t = a.tok[rows, :].astype(f32)
        n = t * lax.rsqrt(jnp.mean(t * t, axis=-1, keepdims=True) + epsilon) * row(a.ng)
        s.normed[rows, :] = n.astype(bf16)
    ready("dtw", "dtb", "alog", "dskip", "wbc")
    wdt_s[0:heads, :] = a.dtw[...]
    for k, name in enumerate(("dtb", "alog", "dskip")):
        hp[k : k + 1, 0:heads] = row(a[name])
    for c in range(chunks):
        rows = pl.ds(c * Q, Q)
        n = s.normed[rows, :]
        bc_o[pl.ds(HEAD + c * Q, Q), :] = mm(n, a.wbc[...])
        s.dt[rows, :] = mm(n, wdt_s[...], NT)
    ready("wx")
    for c in range(chunks):
        x_o[pl.ds(HEAD + c * Q, Q), :] = mm(s.normed[pl.ds(c * Q, Q), :], a.wx[...])
    ready("wz", "wo", "cot")
    for c in range(chunks):
        rows = pl.ds(c * Q, Q)
        s.gate[rows, :] = mm(s.normed[rows, :], a.wz[...])
        s.dgn[rows, :] = mm(a.cot[rows, :], a.wo[...], NT)
    ready("cx", "cxb", "cbc", "cbcb", "gg")
    copies = []
    for c in range(chunks):
        rows = pl.ds(c * Q, Q)
        v = shifted(x_o, c * Q, a.cx, row(a.cxb))
        xc = v * jax.nn.sigmoid(v)
        v = shifted(bc_o, c * Q, a.cbc, row(a.cbcb))
        bcc = v * jax.nn.sigmoid(v)
        b = bcc[:, :states].astype(bf16)
        cc = bcc[:, states:].astype(bf16)
        _, step, _, _, cum = decays(s.dt[rows, :], hp)
        s.cum[rows, :] = cum
        cum_t = jnp.transpose(cum)
        u = xc * exact(step, spread)
        scores = mm(cc, b, NT)
        outs = []
        for g in range(inner // LANES):
            part = u[:, g * LANES : (g + 1) * LANES]
            acc = jnp.zeros((Q, LANES), f32)
            for k in range(per):
                h = g * per + k
                e = jnp.exp(jnp.where(causal, cum[:, h : h + 1] - cum_t[h : h + 1, :], -1e30))
                acc = acc + mm(scores * e, jnp.where(lane // head_dim == k, part, 0.0))
            outs.append(acc)
        mixed = jnp.concatenate(outs, axis=1)
        if c > 0:
            mixed = mixed + mm(cc, state_o[c], NT) * exact(jnp.exp(cum), spread)
        if c + 1 < chunks:
            last = cum[Q - 1 : Q, :]
            tail = u * exact(jnp.exp(last - cum), spread)
            update = mm(tail, b, TN)
            if c > 0:
                rowdec = jnp.sum(
                    spread_rows(inner, head_dim) * jnp.exp(last), axis=1, keepdims=True
                )
                update = update + state_o[c] * rowdec
            state_o[c + 1] = update
        skip = jnp.sum(spread * hp_skip_col(hp), axis=0, keepdims=True)
        mixed = mixed + skip * xc
        s.mixed[rows, :] = mixed
        gate = s.gate[rows, :]
        gated = mixed * (gate * jax.nn.sigmoid(gate))
        sq = jnp.sum(gated * gated, axis=1, keepdims=True)
        pr = jnp.sum(row(a.gg) * s.dgn[rows, :] * gated, axis=1, keepdims=True)
        both = jnp.where(lane == 0, sq, jnp.where(lane == 1, pr, 0.0))
        s.stats[c] = jnp.transpose(both)[0:8, :]
        if c == 0:
            meet()
        copies.append(exchange(s, c, s.stats))
    return copies


def row(ref):
    return ref[...][None, :]


def back(heads, inner_total, a, s, copies, launch, hook):
    length, inner = s.mixed.shape
    states = a.cbc.shape[1] // 2
    head_dim = inner // heads
    per = LANES // head_dim
    taps = a.cx.shape[0]
    chunks = length // Q
    hp, wdt_s = s.hp, s.wdt
    x_r, bc_r = s.x, s.bc
    gn_s, dz_s, dx_s, dbc_s, ddt_s = s.gn, s.dz, s.dx, s.dbc, s.ddt
    dvx_s, dvbc_s = s.dvx, s.dvbc
    cx, cbc = a.cx, a.cbc
    gg = row(a.gg)
    spread = spread_matrix(inner, head_dim)
    spread_r = spread_rows(inner, head_dim)
    causal = iota((Q, Q), 0) >= iota((Q, Q), 1)
    lower = causal.astype(f32)
    lane = iota((Q, LANES), 1)
    skip = jnp.sum(spread * hp_skip_col(hp), axis=0, keepdims=True)
    dvx_s[pl.ds(length, HEAD), :] = jnp.zeros((HEAD, inner), f32)
    dvbc_s[pl.ds(length, HEAD), :] = jnp.zeros((HEAD, 2 * states), f32)
    g_gain = jnp.zeros((1, inner), f32)
    for c in range(chunks):
        rows = pl.ds(c * Q, Q)
        total = s.stats[c]
        for copy, k in copies[c]:
            copy.wait()
            total = total + s.st_slot[k]
        block = jnp.concatenate([total, jnp.zeros((LANES - 8, Q), f32)], axis=0)
        turned = jnp.transpose(block)
        gate = s.gate[rows, :]
        mixed = s.mixed[rows, :]
        sg = jax.nn.sigmoid(gate)
        act = gate * sg
        gated = mixed * act
        inv = lax.rsqrt(turned[:, 0:1] / inner_total + epsilon)
        pm = turned[:, 1:2] / inner_total
        dgn = s.dgn[rows, :]
        normal = gated * inv
        gn_s[rows, :] = (normal * gg).astype(bf16)
        g_gain = g_gain + jnp.sum(dgn * normal, axis=0, keepdims=True)
        dg = inv * (gg * dgn) - gated * (inv * inv * inv) * pm
        s.dy[rows, :] = dg * act
        dz_s[rows, :] = (dg * mixed * (sg * (1.0 + gate * (1.0 - sg)))).astype(bf16)
    s.p_gwo[...] = mm(gn_s[...], a.cot[...], TN).astype(bf16)
    launch("gwo")
    hook()
    s.p_gz[...] = mm(s.normed[...], dz_s[...], TN).astype(bf16)
    launch("gz")
    hook()
    s.p_res[...] = mm(gn_s[...], a.wo[...]).astype(bf16)
    launch("res")
    hook()

    g_skip = jnp.zeros((1, inner), f32)
    g_alog = jnp.zeros((1, LANES), f32)
    g_dtb = jnp.zeros((1, LANES), f32)
    g_cx = [jnp.zeros((1, inner), f32) for _ in range(taps)]
    g_cxb = jnp.zeros((1, inner), f32)
    g_cbc = [jnp.zeros((1, 2 * states), f32) for _ in range(taps)]
    g_cbcb = jnp.zeros((1, 2 * states), f32)
    d_state = None
    for c in reversed(range(chunks)):
        rows = pl.ds(c * Q, Q)
        dy = s.dy[rows, :]
        vx = shifted(x_r, c * Q, cx, row(a.cxb))
        sx = jax.nn.sigmoid(vx)
        xc = vx * sx
        vb = shifted(bc_r, c * Q, cbc, row(a.cbcb))
        sb = jax.nn.sigmoid(vb)
        bcc = vb * sb
        b = bcc[:, :states].astype(bf16)
        cc = bcc[:, states:].astype(bf16)
        pre = s.dt[rows, :] + hp[0:1, :]
        step = softplus(pre)
        rate = jnp.exp(hp[1:2, :])
        log_decay = -step * rate
        cum = s.cum[rows, :]
        cum_t = jnp.transpose(cum)
        stepw = exact(step, spread)
        u = xc * stepw
        scores = mm(cc, b, NT)
        d_scores = jnp.zeros((Q, Q), f32)
        d_cum = jnp.zeros((Q, LANES), f32)
        cols = jnp.zeros((8, Q), f32)
        dus = []
        for g in range(inner // LANES):
            up = u[:, g * LANES : (g + 1) * LANES].astype(bf16)
            dyp = dy[:, g * LANES : (g + 1) * LANES]
            acc = jnp.zeros((Q, LANES), f32)
            for k in range(per):
                h = g * per + k
                e = jnp.exp(jnp.where(causal, cum[:, h : h + 1] - cum_t[h : h + 1, :], -1e30))
                p = scores * e
                dyh = jnp.where(lane // head_dim == k, dyp, 0.0).astype(bf16)
                dp = mm(dyh, up, NT)
                d_scores = d_scores + dp * e
                gp = dp * p
                d_cum = d_cum + jnp.where(lane == h, jnp.sum(gp, axis=1, keepdims=True), 0.0)
                cols = cols + jnp.where(
                    iota((8, Q), 0) == h, jnp.sum(gp, axis=0, keepdims=True), 0.0
                )
                acc = acc + mm(p, dyh, TN)
                hook()
            dus.append(acc)
        du = jnp.concatenate(dus, axis=1)
        d_cum = d_cum - jnp.transpose(
            jnp.concatenate([cols, jnp.zeros((LANES - 8, Q), f32)], axis=0)
        )
        d_c = mm(d_scores, b)
        d_b = mm(d_scores, cc, TN)
        d_prev = None
        if c > 0:
            state = s.state[c]
            decayed = exact(jnp.exp(cum), spread)
            dz = dy * decayed
            carried = mm(cc, state, NT) * dz
            d_cum = d_cum + exact(carried, spread, NT)
            d_c = d_c + mm(dz, state)
            d_prev = mm(dz, cc, TN)
        if d_state is not None:
            last = cum[Q - 1 : Q, :]
            tailw = exact(jnp.exp(last - cum), spread)
            ut = u * tailw
            dut = mm(b, d_state, NT)
            d_b = d_b + mm(ut, d_state)
            du = du + dut * tailw
            q = exact(dut * ut, spread, NT)
            d_last = jnp.sum(q, axis=0, keepdims=True)
            if c > 0:
                rowdec = jnp.sum(spread_r * jnp.exp(last), axis=1, keepdims=True)
                r = jnp.sum(d_state * s.state[c], axis=1, keepdims=True) * rowdec
                d_last = d_last + jnp.sum(spread_r * r, axis=0, keepdims=True)
                d_prev = d_prev + d_state * rowdec
            d_cum = d_cum - q + jnp.where(iota((Q, LANES), 0) == Q - 1, d_last, 0.0)
        d_state = d_prev
        d_log = exact(lower, d_cum, TN)
        g_alog = g_alog + jnp.sum(d_log * log_decay, axis=0, keepdims=True)
        d_step = exact(du * xc, spread, NT) - d_log * rate
        d_pre = d_step * jax.nn.sigmoid(pre)
        d_pre = jnp.where(lane < heads, d_pre, 0.0)
        g_dtb = g_dtb + jnp.sum(d_pre, axis=0, keepdims=True)
        g_skip = g_skip + jnp.sum(dy * xc, axis=0, keepdims=True)
        dxc = du * stepw + skip * dy
        dvx = dxc * (sx * (1.0 + vx * (1.0 - sx)))
        dvb = jnp.concatenate([d_b, d_c], axis=1) * (sb * (1.0 + vb * (1.0 - sb)))
        dvx_s[rows, :] = dvx
        dvbc_s[rows, :] = dvb
        g_cxb = g_cxb + jnp.sum(dvx, axis=0, keepdims=True)
        g_cbcb = g_cbcb + jnp.sum(dvb, axis=0, keepdims=True)
        dx = jnp.zeros((Q, inner), f32)
        dbc = jnp.zeros((Q, 2 * states), f32)
        for j in range(taps):
            behind = pl.ds(c * Q + taps - 1 - j, Q)
            ahead = pl.ds(HEAD + c * Q - taps + 1 + j, Q)
            dx = dx + cx[j : j + 1, :] * dvx_s[behind, :]
            dbc = dbc + cbc[j : j + 1, :] * dvbc_s[behind, :]
            g_cx[j] = g_cx[j] + jnp.sum(dvx * x_r[ahead, :], axis=0, keepdims=True)
            g_cbc[j] = g_cbc[j] + jnp.sum(dvb * bc_r[ahead, :], axis=0, keepdims=True)
        dx_s[rows, :] = dx.astype(bf16)
        dbc_s[rows, :] = dbc.astype(bf16)
        ddt_s[rows, :] = d_pre.astype(bf16)
        hook()

    normed = s.normed
    s.p_gbc[...] = mm(normed[...], dbc_s[...], TN).astype(bf16)
    launch("gbc")
    hook()
    s.p_gx[...] = mm(normed[...], dx_s[...], TN).astype(bf16)
    launch("gx")
    hook()
    g_ng = jnp.zeros((1, normed.shape[1]), f32)
    for c in range(chunks):
        rows = pl.ds(c * Q, Q)
        dn = mm(dz_s[rows, :], a.wz[...], NT) + mm(dx_s[rows, :], a.wx[...], NT)
        dn = dn + mm(dbc_s[rows, :], a.wbc[...], NT) + mm(ddt_s[rows, :], wdt_s[...])
        s.p_dn[rows, :] = dn.astype(bf16)
        t = a.tok[rows, :].astype(f32)
        unit = t * lax.rsqrt(jnp.mean(t * t, axis=-1, keepdims=True) + epsilon)
        g_ng = g_ng + jnp.sum(dn * unit, axis=0, keepdims=True)
        if c == 0:
            hook()
    launch("dn")
    hook()
    gdt = mm(ddt_s[...], normed[...], TN)
    small = s.p_sm
    small[...] = jnp.zeros(small.shape, f32)
    at = put_rows(small, 0, gdt[0:heads, :])
    for value in (*g_cx, g_cxb, g_gain, g_dtb, g_alog, exact(g_skip, spread, NT)):
        at = put_rows(small, at, value)
    at = -(-at // 8) * 8
    for value in (*g_cbc, g_cbcb, g_ng):
        at = put_rows(small, at, value)
    launch("sm")


INPUTS = (
    "tok", "cot", "ng", "wz", "wx", "wbc", "dtw", "cx", "cxb", "cbc", "cbcb",
    "dtb", "alog", "dskip", "gg", "wo",
)
FETCH = (
    "tok", "ng", "dtw", "dtb", "alog", "dskip", "wbc", "wx", "wz", "wo", "cot",
    "cx", "cxb", "cbc", "cbcb", "gg",
)
RESULTS = ("res", "dn", "gz", "gx", "gwo", "gbc", "sm")


def kernel_main(heads, inner_total, sc, plan, hooks, bits, *refs):
    hbm = dict(zip(INPUTS, refs))
    outs = dict(zip(RESULTS, refs[len(INPUTS) :]))
    s = sc.bind(refs[len(INPUTS) + len(RESULTS) :])
    at = Place()
    a = Refs((name, s["a_" + name]) for name in INPUTS)
    loads = {}
    for k, name in enumerate(FETCH):
        loads[name] = pltpu.make_async_copy(hbm[name], a[name], s.loads.at[k])
        loads[name].start()
    meet = greet(at, bits)

    def ready(*names):
        for name in names:
            loads[name].wait()

    running = {}

    def launch(name):
        for k, (stream, source, start, rows) in enumerate(plan):
            if source == name:
                part = s["o_" + name].at[pl.ds(start, rows), :]
                run = stream.run(s, at, s["p_" + name].at[pl.ds(start, rows), :], part)
                store = pltpu.make_async_copy(
                    part, outs[name].at[pl.ds(start, rows), :], s.stores.at[k]
                )
                running[k] = (run, store)

    stores = []

    def advance(k):
        if k in running and next(running[k][0], 1) is not None:
            store = running.pop(k)[1]
            store.start()
            stores.append(store)

    turn = iter(hooks)

    def hook():
        for k in next(turn, ()):
            advance(k)

    copies = front(heads, a, s, ready, meet)
    back(heads, inner_total, a, s, copies, launch, hook)
    for ks in turn:
        for k in ks:
            advance(k)
    while running:
        for k in list(running):
            advance(k)
    for store in stores:
        store.wait()


SUMS = ("tok", "cot", "ng", *RESULTS)
FINAL = (
    "res", "gt", "ng", "gz", "gx", "gbc", "gdt", "cx", "cxb", "cbc", "cbcb",
    "dtb", "alog", "skip", "gain", "gwo",
)


def kernel_finish(sc, *refs):
    count = len(SUMS) + len(FINAL)
    s = sc.bind(refs[count:])
    loads = {}
    for k, name in enumerate(("gwo", "gz", "gx", "gbc", "sm", "tok", "cot", "ng", "res", "dn")):
        loads[name] = pltpu.make_async_copy(
            refs[SUMS.index(name)], s["i_" + name], s.loads.at[k]
        )
        loads[name].start()
    stores = []

    def store(*names):
        for name in names:
            k = FINAL.index(name)
            copy = pltpu.make_async_copy(s["o_" + name], refs[len(SUMS) + k], s.stores.at[k])
            copy.start()
            stores.append(copy)

    for name in ("gwo", "gz", "gx", "gbc"):
        loads[name].wait()
        s["o_" + name][...] = s["i_" + name][...].astype(f32)
        store(name)
    loads["sm"].wait()
    sums = s.i_sm
    at = 0
    for name in ("gdt", "cx"):
        out = s["o_" + name]
        for r in range(out.shape[0]):
            out[r : r + 1, :] = get_row(sums, at, out.shape[1])
            at += out.shape[1] // LANES
    for name in ("cxb", "gain"):
        out = s["o_" + name]
        out[...] = get_row(sums, at, out.shape[0])[0]
        at += out.shape[0] // LANES
    for name in ("dtb", "alog", "skip"):
        out = s["o_" + name]
        out[...] = sums[at, 0 : out.shape[0]]
        at += 1
    at = -(-at // 8) * 8
    out = s.o_cbc
    for r in range(out.shape[0]):
        out[r : r + 1, :] = get_row(sums, at, out.shape[1])
        at += out.shape[1] // LANES
    for name in ("cbcb", "ng"):
        out = s["o_" + name]
        out[...] = get_row(sums, at, out.shape[0])[0]
        at += out.shape[0] // LANES
    store("gdt", "cx", "cxb", "gain", "dtb", "alog", "skip", "cbc", "cbcb", "ng")
    for name in ("tok", "cot", "ng", "res", "dn"):
        loads[name].wait()
    for c in range(s.i_tok.shape[0] // Q):
        rows = pl.ds(c * Q, Q)
        t = s.i_tok[rows, :].astype(f32)
        s.o_res[rows, :] = (t + s.i_res[rows, :].astype(f32)).astype(bf16)
        r = lax.rsqrt(jnp.mean(t * t, axis=-1, keepdims=True) + epsilon)
        gd = s.i_dn[rows, :].astype(f32) * row(s.i_ng)
        mean = jnp.mean(t * gd, axis=-1, keepdims=True)
        d = r * gd - t * (r * r * r) * mean
        s.o_gt[rows, :] = (s.i_cot[rows, :].astype(f32) + d).astype(bf16)
    store("res", "gt")
    for copy in stores:
        copy.wait()


KINDS = {"P": PairFirst, "Q": LineFirst}
PATHS = {
    "gwo": "PPQPPQ",
    "gz": "PPPP",
    "gx": "PPQQ",
}
ORDER = (
    (0, 2,),
    (1,),
    (14,),
    (3, 5,),
    (),
    (4,),
    (14, 6, 0,),
    (1, 2,),
    (7,),
    (3,),
    (),
    (8, 4, 5,),
    (),
    (0, 2,),
    (6, 1,),
    (9,),
    (3, 7,),
    (16,),
    (10, 5,),
    (12, 4, 8, 0,),
    (15, 16, 2, 6, 1,),
    (17, 3, 9, 7, 14, 10, 4, 15, 0, 17, 5, 12,),
    (2, 14, 16, 1, 8, 0, 6, 3, 13, 9, 7, 4,),
    (1, 5, 16, 10, 3, 11, 2, 12, 4, 6, 8, 13,),
    (7, 16, 9, 11, 15, 5, 17, 6, 10, 12, 8, 15,),
    (7, 13, 11, 9, 16, 10, 17, 8, 12, 9, 11, 17,),
    (16, 13, 10, 12, 17, 16, 11, 13, 17, 11, 16, 17,),
    (13, 16,),
)


def call(body, args, outs, scratch=(), **params):
    hbm = pl.BlockSpec(memory_space=pltpu.HBM)
    return pl.pallas_call(
        body,
        out_shape=[jax.ShapeDtypeStruct(s, d) for s, d in outs],
        in_specs=[hbm] * len(args),
        out_specs=[hbm] * len(outs),
        scratch_shapes=list(scratch),
        compiler_params=pltpu.CompilerParams(vmem_limit_bytes=63 * 1024 * 1024, **params),
    )(*args)


def per_device(
    tokens, cotangent, norm_gain, w_z, w_x, w_bc, w_dt, conv_x, conv_x_bias, conv_bc,
    conv_bc_bias, dt_bias, a_log, d_skip, gate_gain, w_out,
):
    seqs, length, width = tokens.shape
    assert seqs == 1 and length % Q == 0
    heads = dt_bias.shape[0]
    inner = w_z.shape[1]
    wide = w_bc.shape[1]
    states = wide // 2
    taps = conv_x.shape[0]
    dp, tensor = lax.axis_size("dp"), lax.axis_size("tensor")
    assert dp % 4 == 0 and tensor & (tensor - 1) == 0
    inner_total = inner * tensor
    chunks = length // Q
    tok = tokens.reshape(length, width)
    cot = cotangent.reshape(length, width)
    args = (
        tok, cot, norm_gain, w_z, w_x, w_bc, w_dt.T, conv_x, conv_x_bias, conv_bc,
        conv_bc_bias, dt_bias, a_log, d_skip, gate_gain, w_out,
    )
    bits = [("tensor", 1 << k) for k in range(tensor.bit_length() - 1)]
    sc = Scratch()
    for name, value in zip(INPUTS, args):
        sc.vmem("a_" + name, value.shape, value.dtype)
    sc.dma("loads", len(INPUTS))
    sc.vmem("wdt", (LANES, width), bf16)
    sc.vmem("hp", (8, LANES))
    sc.vmem("normed", (length, width), bf16)
    for name in ("gate", "mixed", "dgn", "dy"):
        sc.vmem(name, (length, inner))
    for name in ("x", "dvx"):
        sc.vmem(name, (length + HEAD, inner))
    for name in ("bc", "dvbc"):
        sc.vmem(name, (length + HEAD, wide))
    for name in ("dt", "cum"):
        sc.vmem(name, (length, LANES))
    sc.vmem("state", (chunks, inner, states))
    sc.vmem("stats", (chunks, 8, Q))
    sc.vmem("st_slot", (chunks * (tensor - 1), 8, Q))
    sc.dma("st_s", chunks * (tensor - 1))
    sc.dma("st_r", chunks * (tensor - 1))
    for name in ("gn", "dz", "dx"):
        sc.vmem(name, (length, inner), bf16)
    sc.vmem("dbc", (length, wide), bf16)
    sc.vmem("ddt", (length, LANES), bf16)
    own_rows = heads * width // LANES + (taps + 2) * inner // LANES + 3
    own_rows = -(-own_rows // 8) * 8
    all_rows = (taps + 1) * wide // LANES + width // LANES
    all_rows = -(-(own_rows + all_rows) // 16) * 16 - own_rows
    results = [
        ((length, width), bf16),
        ((length, width), bf16),
        ((width, inner), bf16),
        ((width, inner), bf16),
        ((inner, width), bf16),
        ((width, wide), bf16),
        ((own_rows + all_rows, LANES), f32),
    ]
    for name, (shape, dtype) in zip(RESULTS, results):
        sc.vmem("p_" + name, shape, dtype)
        sc.vmem("o_" + name, shape, dtype)
    plan = []

    def split(name, kinds):
        shape, dtype = results[RESULTS.index(name)]
        rows = shape[0] // len(kinds)
        for k, kind in enumerate(kinds):
            plan.append((kind(sc, f"{name}{k}", rows, shape[1], dtype), name, k * rows, rows))

    split("gwo", [KINDS[k] for k in PATHS["gwo"]])
    split("gz", [KINDS[k] for k in PATHS["gz"]])
    split("gx", [KINDS[k] for k in PATHS["gx"]])
    for name in ("res", "dn"):
        shape, dtype = results[RESULTS.index(name)]
        plan.append((Halves(sc, name, *shape, dtype, bits), name, 0, shape[0]))
    plan.append((Nested(sc, "gbc", width, wide, bf16, bits, PairFirst), "gbc", 0, width))
    plan.append((Small(sc, "sm", own_rows, LANES, all_rows, bits), "sm", 0, own_rows + all_rows))
    sc.dma("stores", len(plan))
    sums = call(
        functools.partial(kernel_main, heads, inner_total, sc, plan, ORDER, bits),
        args,
        results,
        sc.shapes,
        collective_id=0,
        has_side_effects=True,
    )
    final = [
        ((length, width), bf16),
        ((length, width), bf16),
        ((width,), f32),
        ((width, inner), f32),
        ((width, inner), f32),
        ((width, wide), f32),
        ((heads, width), f32),
        ((taps, inner), f32),
        ((inner,), f32),
        ((taps, wide), f32),
        ((wide,), f32),
        ((heads,), f32),
        ((heads,), f32),
        ((heads,), f32),
        ((inner,), f32),
        ((inner, width), f32),
    ]
    last = Scratch()
    sources = (tok, cot, norm_gain, *sums)
    for name, value in zip(SUMS, sources):
        last.vmem("i_" + name, value.shape, value.dtype)
    for name, (shape, dtype) in zip(FINAL, final):
        last.vmem("o_" + name, shape, dtype)
    last.dma("loads", len(SUMS))
    last.dma("stores", len(FINAL))
    outs = call(functools.partial(kernel_finish, last), sources, final, last.shapes)
    outs = list(outs)
    for k in range(2):
        outs[k] = outs[k].reshape(seqs, length, width)
    outs[6] = outs[6].T
    return tuple(outs)


def solution(mesh):
    placed = (
        P("dp", None, None),
        P("dp", None, None),
        P(),
        P(None, "tensor"),
        P(None, "tensor"),
        P(),
        P(None, "tensor"),
        P(None, "tensor"),
        P("tensor"),
        P(),
        P(),
        P("tensor"),
        P("tensor"),
        P("tensor"),
        P("tensor"),
        P("tensor", None),
    )
    return jax.shard_map(
        per_device,
        mesh=mesh,
        in_specs=placed,
        out_specs=(
            P("dp", None, None),
            P("dp", None, None),
            P(),
            P(None, "tensor"),
            P(None, "tensor"),
            P(),
            P(None, "tensor"),
            P(None, "tensor"),
            P("tensor"),
            P(),
            P(),
            P("tensor"),
            P("tensor"),
            P("tensor"),
            P("tensor"),
            P("tensor", None),
        ),
        check_vma=False,
    )
```
